32 devices in a mesh: groups: 2 (over x), pairs: 16 (over z, y, core).
Axes of the slice: x: 2, y: 2, z: 4, core: 2. Of those that a mesh axis runs over, the one named last changes fastest.
Arguments:
- traces: bfloat16 [128, 3, 4096], P(('groups', 'pairs')), parts along dimension 0, may hold values from -6 to 6
- gaps: int32 [128, 2], P(('groups', 'pairs')), parts along dimension 0, may hold values 0 or 1
- assign: int32 [128], P('groups'), parts along dimension 0, may hold values from 0 to 3, as said below
- target: int32 [32], P('groups'), parts along dimension 0, may hold values from 0 to 3, as said below
Outputs:
- correlations: bfloat16 [128, 16, 2, 9, 256], P(('groups', 'pairs')), parts along dimension 0
- energy: float32 [128, 9], P(('groups', 'pairs')), parts along dimension 0
The draws below stay inside these ranges and needn't reach their ends.
There are 2 independent parts, one for each index of `groups`. The reference program is written for one: setup_inputs(seed, part) draws one part's arguments, and reference() takes and returns one part's arrays. A program takes and returns all parts, laid end to end along the dimension named above; each array names one. Nothing has to cross between parts.
Inputs may be any that keep to these rules, and one draw needn't show every extreme that they name: `assign`: the 4 stations of one owner name at most 2 stations of any block; in every draw one block takes exactly 2 stations of every owner. `target`: in every draw some owner names the block that takes 2 stations of every owner.
All inputs are finite; a program needn't handle non-finite values. No bound on the sum of `gaps` on one device may be relied on, other than what follows from the above.
Results may differ from the reference program's by a relative error of at most 0.0075.
Values may be sent and summed in bfloat16 or wider, within the bound.
No kernel may reach another device: no remote copies, remote signals or barrier semaphores. Data moves between devices by JAX's collectives and lax.ppermute only.
A program may use at most 128 MiB of HBM per device.

```python
import math
import jax
import jax.numpy as jnp
from jax import lax

STA_DEV = 4
WINDOWS = 2
SEG = 2048
FREQ = 512
FLO = 64
LAGS = 256
HALF = 21
CAP = 2
BLOCKS = 4
OWNERS = 16
STATIONS = 64
N_PAIRS = 16


def block_plan(key):
    base = jax.random.fold_in(key, 4242)
    hot_key, owner_key, target_key, holder_key = jax.random.split(base, 4)
    hottest = jax.random.randint(hot_key, (), 0, BLOCKS)
    others = jnp.arange(BLOCKS - 1, dtype=jnp.int32)
    others = jnp.where(others >= hottest, others + 1, others)
    pool = jnp.repeat(others, CAP)

    def one_owner(owner_seed):
        first_seed, second_seed = jax.random.split(owner_seed)
        chosen = jax.random.permutation(first_seed, pool)[:STA_DEV - CAP]
        filled = jnp.concatenate([jnp.full((CAP,), hottest, jnp.int32), chosen.astype(jnp.int32)])
        return jax.random.permutation(second_seed, filled)
    assigned = jax.vmap(one_owner)(jax.random.split(owner_key, OWNERS)).reshape(-1)
    targets = jax.random.randint(target_key, (OWNERS,), 0, BLOCKS)
    holder = jax.random.randint(holder_key, (), 0, OWNERS)
    targets = jnp.where(jnp.arange(OWNERS) == holder, hottest, targets)
    return (assigned.astype(jnp.int32), targets.astype(jnp.int32))


def draw_assign(key, part):
    return block_plan(key)[0]


def draw_target(key, part):
    return block_plan(key)[1]


def with_ends(values, rng, least, largest):
    index_at = [jax.random.randint(jax.random.fold_in(rng, axis), (), 0, length) for axis, length in enumerate(values.shape)]
    main_axis = values.shape.index(max(values.shape))
    beside = index_at[:main_axis] + [(index_at[main_axis] + 1) % values.shape[main_axis]] + index_at[main_axis + 1:]
    return values.at[tuple(index_at)].set(least).at[tuple(beside)].set(largest)


def shard_levels(key, shape, shards, low, top_value):
    def one(axis_at, parts):
        draws = jax.random.uniform(jax.random.fold_in(jax.random.fold_in(key, 6), axis_at), (parts,), jnp.float32, low / len(shards), top_value / len(shards))
        return jnp.repeat(jnp.exp(draws), shape[axis_at] // parts).reshape((-1,) + (1,) * (len(shape) - axis_at - 1))

    level = one(*shards[0])
    for cut in shards[1:]:
        level = level * one(*cut)
    return level


def normal_values(key, shape, width, bound, pieces=(), kind=jnp.bfloat16):
    array = width * jax.random.normal(key, shape, jnp.float32)
    if pieces:
        array = array * shard_levels(key, shape, pieces, -0.22, 0.18)
    return jnp.clip(array, -bound, bound).astype(kind)


def setup_inputs(seed: int = 0, part: int = 0) -> dict:
    arg_keys = jax.random.split(jax.random.key(seed), 5)
    part_keys = jax.random.split(jax.random.fold_in(arg_keys[4], part), 5)
    return {
        "traces": normal_values(part_keys[0], (STATIONS, 3, WINDOWS * SEG), 1.0, 6.0, ((0, 16),)),
        "gaps": with_ends((jax.random.randint(part_keys[1], (STATIONS, WINDOWS), 0, 4) < 3).astype(jnp.int32), jax.random.fold_in(part_keys[1], 1), 0, 1),
        "assign": draw_assign(jax.random.fold_in(jax.random.fold_in(arg_keys[4], part), 71), part),
        "target": draw_target(jax.random.fold_in(jax.random.fold_in(arg_keys[4], part), 71), part),
    }


def dft_table():
    samples = jnp.arange(SEG, dtype=jnp.int32)[:, None]
    bins = FLO + jnp.arange(FREQ, dtype=jnp.int32)[None, :]
    phase = jnp.mod(samples * bins, SEG).astype(jnp.float32) * (2.0 * math.pi / SEG)
    return jnp.concatenate([jnp.cos(phase), -jnp.sin(phase)], axis=1).astype(jnp.bfloat16)

def lag_table():
    bins = FLO + jnp.arange(FREQ, dtype=jnp.int32)[:, None]
    shifts = jnp.arange(LAGS, dtype=jnp.int32)[None, :] - LAGS // 2
    phase = jnp.mod(bins * shifts, SEG).astype(jnp.float32) * (2.0 * math.pi / SEG)
    return jnp.concatenate([jnp.cos(phase), -jnp.sin(phase)], axis=0).astype(jnp.bfloat16)

def smooth_band():
    column = jnp.arange(FREQ, dtype=jnp.int32)
    band = (jnp.abs(column[:, None] - column[None, :]) <= HALF).astype(jnp.float32)
    return (band, lax.optimization_barrier(jnp.sum(band, axis=0)))

def whiten_all(traces, gaps):
    stations = traces.shape[0]
    windows = gaps.shape[1]
    segments = traces.reshape(stations * 3 * windows, SEG)
    spectra = jnp.dot(segments, dft_table(), preferred_element_type=jnp.float32)
    spectra = spectra.reshape(stations, 3, windows, 2, FREQ)
    power = lax.optimization_barrier(jnp.sum(spectra * spectra, axis=(1, 3))) / 3.0
    band, bin_count = smooth_band()
    smooth = jnp.dot(power.reshape(-1, FREQ), band, precision=lax.Precision.HIGHEST)
    smooth = smooth.reshape(stations, windows, FREQ) / bin_count
    factor = gaps.astype(jnp.float32)[:, :, None] / jnp.sqrt(smooth + 1e-06)
    return (spectra * factor[:, None, :, None, :]).astype(jnp.bfloat16)

def station_ranks(owner_assign):
    own_count = owner_assign.shape[1]
    same = owner_assign[:, :, None] == owner_assign[:, None, :]
    order = jnp.arange(own_count, dtype=jnp.int32)
    before = order[:, None] < order[None, :]
    return lax.optimization_barrier(jnp.sum((same & before[None, :, :]).astype(jnp.int32), axis=1))

def correlate_block(whitened, own_mask, partner, partner_mask):
    own_count = whitened.shape[0]
    slot_count = partner.shape[0]
    real_part = partner[:, :, :, 0]
    imag_part = partner[:, :, :, 1]
    quad = jnp.stack([jnp.stack([real_part, imag_part], 3), jnp.stack([-imag_part, real_part], 3)], 4)
    cross = jnp.einsum('icwrf,jdwrof->ijcdof', whitened.astype(jnp.float32), quad.astype(jnp.float32))
    cross = cross.astype(jnp.bfloat16)
    lagged = jnp.dot(cross.reshape(-1, 2 * FREQ), lag_table(), preferred_element_type=jnp.float32)
    lagged = lagged.reshape(own_count, slot_count, 9, LAGS)
    counts = jnp.dot(own_mask, partner_mask.T, precision=lax.Precision.HIGHEST)
    scale = 1.0 / (jnp.maximum(counts, 1.0) * math.sqrt(FREQ))
    return (lagged * scale[:, :, None, None]).astype(jnp.bfloat16)

def reference(traces, gaps, assign, target):
    owners = N_PAIRS
    own_count = STA_DEV
    windows = gaps.shape[1]
    whitened = whiten_all(traces, gaps).reshape(owners, own_count, 3, windows, 2, FREQ)
    masks = gaps.astype(jnp.float32).reshape(owners, own_count, windows)
    owner_assign = assign.reshape(owners, own_count)
    ranks = station_ranks(owner_assign)
    flat_rows = whitened.reshape(owners, own_count, -1).astype(jnp.float32)
    slot_ids = jnp.arange(CAP, dtype=jnp.int32)

    def per_owner(inputs):
        own_white, own_mask, wanted = inputs
        selection = ((owner_assign == wanted)[:, None, :] & (ranks[:, None, :] == slot_ids[None, :, None])).astype(jnp.float32)
        partner = jnp.einsum('ecs,esr->ecr', selection, flat_rows).astype(jnp.bfloat16)
        partner_mask = jnp.einsum('ecs,esw->ecw', selection, masks)
        block = correlate_block(own_white, own_mask, partner.reshape(owners * CAP, 3, windows, 2, FREQ), partner_mask.reshape(owners * CAP, windows))
        slot_energy = lax.optimization_barrier(jnp.sum(jnp.square(block.astype(jnp.float32)), axis=(0, 3))).reshape(owners, CAP, 9)
        share = jnp.einsum('ecs,ecq->esq', selection, slot_energy, precision=lax.Precision.HIGHEST)
        return (block.reshape(own_count, owners, CAP, 9, LAGS), share)
    blocks, shares = lax.map(per_owner, (whitened, masks, target))
    energy = lax.optimization_barrier(jnp.sum(shares, axis=0)).reshape(owners * own_count, 9) / float(owners * LAGS)
    return (blocks.reshape(owners * own_count, owners, CAP, 9, LAGS), energy)
```

```python
import functools
import math

import jax
import jax.numpy as jnp
import numpy as np
from jax import lax
from jax.experimental import pallas as pl
from jax.experimental.pallas import tpu as pltpu
from jax.sharding import PartitionSpec as P

SEG = 2048
FREQ = 512
FLO = 64
LAGS = 256
HALF = 21
CAP = 2
COMP = 3
RADIX = 4
LANE = 128
NONE = -1000
PART = SEG // RADIX
PLANE = 2 * COMP * FREQ
WIDE = PLANE + LANE
GROUP = 4


def bin_order():
    spot = np.arange(FREQ)
    return RADIX * (spot % LANE) + spot // LANE


def dft_table():
    n1 = np.arange(PART)[:, None]
    blocks = []
    for r in (0, 2, 1, 3):
        k = FLO + RADIX * np.arange(LANE)[None, :] + r
        phase = np.mod(n1 * k, SEG) * (2.0 * math.pi / SEG)
        c, s = np.cos(phase), np.sin(phase)
        blocks.append(np.concatenate([c, -s], 1))
        if r == 1:
            blocks.append(np.concatenate([-s, -c], 1))
        if r == 3:
            blocks.append(np.concatenate([s, c], 1) * np.array([1.0]))
    return np.concatenate(blocks, 0).astype(jnp.bfloat16)


def band_table():
    f = bin_order()
    band = np.abs(f[:, None] - f[None, :]) <= HALF
    share = 1.0 / (float(COMP) * band.sum(0, keepdims=True))
    return band.astype(jnp.bfloat16), share.astype(np.float32)


def lag_table():
    bins = FLO + bin_order()[:, None]
    shifts = np.arange(LAGS)[None, :] - LAGS // 2
    phase = np.mod(bins * shifts, SEG) * (2.0 * math.pi / SEG)
    return np.concatenate([np.cos(phase), -np.sin(phase)], 0).astype(jnp.bfloat16)


def mm(a, b):
    return jnp.dot(a, b, preferred_element_type=jnp.float32)


def front_kernel(gaps_ref, x_ref, tab_ref, band_ref, share_ref, out_ref):
    windows, own = gaps_ref.shape
    rows = windows * own
    quarter = []
    for j in range(RADIX):
        per_comp = []
        for a in range(COMP):
            pieces = [
                x_ref[a, :, w * SEG + j * PART : w * SEG + (j + 1) * PART].astype(jnp.float32)
                for w in range(windows)
            ]
            per_comp.append(jnp.concatenate(pieces, 0))
        quarter.append(jnp.concatenate(per_comp, 0))
    x0, x1, x2, x3 = quarter
    even, odd = x0 + x2, x1 + x3

    def halves(y):
        low = y - y.astype(jnp.bfloat16).astype(jnp.float32)
        return jnp.concatenate([y, low], 0).astype(jnp.bfloat16)

    zero, two = halves(even + odd), halves(even - odd)
    u, v = halves(x0 - x2), halves(x1 - x3)
    tab = lambda i: tab_ref[i * PART : (i + 1) * PART, :]
    both = [
        mm(zero, tab(0)),
        mm(u, tab(2)) + mm(v, tab(3)),
        mm(two, tab(1)),
        mm(u, tab(4)) + mm(v, tab(5)),
    ]
    count = COMP * rows
    spec = [d[:count] + d[count:] for d in both]
    power = []
    for d in spec:
        total = jnp.zeros((rows, LANE), jnp.float32)
        for a in range(COMP):
            re = d[a * rows : (a + 1) * rows, :LANE]
            im = d[a * rows : (a + 1) * rows, LANE:]
            total = total + (re * re + im * im)
        power.append(total)
    power = jnp.concatenate(power, 1)
    p1 = power.astype(jnp.bfloat16).astype(jnp.float32)
    rest = power - p1
    p2 = rest.astype(jnp.bfloat16).astype(jnp.float32)
    p3 = rest - p2
    sums = mm(jnp.concatenate([p1, p2, p3], 0).astype(jnp.bfloat16), band_ref[...])
    smooth = (sums[:rows] + sums[rows : 2 * rows] + sums[2 * rows :]) * share_ref[...]
    row_at = lax.broadcasted_iota(jnp.int32, (rows, LANE), 0)
    flags = jnp.zeros((rows, LANE), jnp.float32)
    for w in range(windows):
        for s in range(own):
            flags = jnp.where(row_at == w * own + s, gaps_ref[w, s].astype(jnp.float32), flags)
    wide_flags = jnp.concatenate([flags] * RADIX, 1)
    factor = wide_flags / jnp.sqrt(smooth + 1e-06)
    for a in range(COMP):
        for part in range(2):
            whole = jnp.concatenate(
                [d[a * rows : (a + 1) * rows, part * LANE : (part + 1) * LANE] for d in spec], 1
            )
            start = (2 * a + part) * FREQ
            out_ref[:, start : start + FREQ] = (whole * factor).astype(jnp.bfloat16)
    out_ref[:, PLANE:] = flags.astype(jnp.bfloat16)


def front(traces, gaps):
    own, comps, length = traces.shape
    windows = gaps.shape[1]
    assert comps == COMP and length == windows * SEG
    band, share = band_table()
    vmem = pl.BlockSpec(memory_space=pltpu.VMEM)
    return pl.pallas_call(
        front_kernel,
        out_shape=jax.ShapeDtypeStruct((windows * own, WIDE), jnp.bfloat16),
        in_specs=[pl.BlockSpec(memory_space=pltpu.SMEM)] + [vmem] * 4,
        out_specs=vmem,
        name="front",
    )(
        gaps.T,
        traces.transpose(1, 0, 2),
        jnp.asarray(dft_table()),
        jnp.asarray(band),
        jnp.asarray(share),
    )


def exchange_masks(count):
    bits = int(count).bit_length() - 1
    assert count == 1 << bits and bits >= 3
    chips = [1 << b for b in range(bits - 1, 0, -1)]
    return [chips + [1], chips + [1]]


def slot_masks(masks):
    found = [0]
    for m in masks:
        found = found + [f ^ m for f in found]
    return found


def correlate_kernel(
    owners, own_rows, windows, assign_ref, target_ref, order_ref, all_ref, lag_ref, out_ref, energy_ref,
    self_f32, picked, pickx, picky, cross, result, outv, acc, sem,
):
    own = own_rows // windows
    me = lax.axis_index("pairs")
    chunk_rows = GROUP * own_rows
    pairs = GROUP * CAP
    stations = GROUP * own
    half = own * COMP * COMP * pairs
    self_f32[...] = all_ref[0:own_rows, :].astype(jnp.float32)
    acc[...] = jnp.zeros_like(acc)
    my_target = target_ref[me]

    def first_two(flags):
        found = [jnp.int32(NONE)] * CAP
        seen = jnp.int32(0)
        for s, flag in enumerate(flags):
            for c in range(CAP):
                found[c] = jnp.where(jnp.logical_and(flag, seen == c), s, found[c])
            seen = seen + flag.astype(jnp.int32)
        return found

    def one_chunk(ch, carry):
        slot = lax.rem(ch, 2)
        ids = [order_ref[ch * GROUP + j] for j in range(GROUP)]
        theirs, mine, yours = [], [], []
        for j in range(GROUP):
            theirs.append(first_two([assign_ref[ids[j] * own + s] == my_target for s in range(own)]))
            want = target_ref[ids[j]]
            mine.append(first_two([assign_ref[me * own + s] == want for s in range(own)]))
        chunk = all_ref[pl.ds(pl.multiple_of(ch * chunk_rows, chunk_rows), chunk_rows), :]

        def one_hot(row_count, cols, want):
            col = lax.broadcasted_iota(jnp.int32, (row_count, cols), 1)
            return jnp.where(col == want, 1.0, 0.0).astype(jnp.bfloat16)

        def iota(row_count, cols):
            return lax.broadcasted_iota(jnp.int32, (row_count, cols), 0)

        row = iota(windows * pairs, chunk_rows)
        within = row % pairs
        want = jnp.full(row.shape, NONE, jnp.int32)
        for j in range(GROUP):
            for c in range(CAP):
                want = jnp.where(within == j * CAP + c, theirs[j][c] + j * own_rows, want)
        sel = one_hot(windows * pairs, chunk_rows, want + (row // pairs) * own)
        row = iota(windows * stations, chunk_rows)
        within = row % stations
        want = (within // own) * own_rows + (row // stations) * own + within % own
        selx = one_hot(windows * stations, chunk_rows, want)
        moved = mm(jnp.concatenate([sel, selx], 0), chunk)
        picked[...] = moved[: windows * pairs]
        pickx[...] = moved[windows * pairs :]
        row = iota(CAP * windows * stations, own_rows)
        within = row % stations
        place = (row // (windows * stations)) * GROUP + within // own
        want = jnp.full(row.shape, NONE, jnp.int32)
        for c in range(CAP):
            for j in range(GROUP):
                want = jnp.where(place == c * GROUP + j, mine[j][c], want)
        w_at = (row // stations) % windows
        sely = one_hot(CAP * windows * stations, own_rows, want + w_at * own)
        picky[...] = mm(sely, all_ref[0:own_rows, :])

        def plane(a, part, lt):
            start = (2 * a + part) * FREQ + lt * LANE
            return pl.ds(pl.multiple_of(start, LANE), LANE)

        def product(left, right):
            re = im = None
            for w in range(windows):
                lr, li = left[w]
                rr, ri = right[w]
                r = lr * rr + li * ri
                i = li * rr - lr * ri
                re = r if re is None else re + r
                im = i if im is None else im + i
            return re, im

        def one_tile(lt, carry):
            re_at = pl.ds(pl.multiple_of(lt * LANE, LANE), LANE)
            im_at = pl.ds(pl.multiple_of(FREQ + lt * LANE, LANE), LANE)
            slots = [
                [
                    [picked[w * pairs : (w + 1) * pairs, plane(b, part, lt)] for part in range(2)]
                    for w in range(windows)
                ]
                for b in range(COMP)
            ]
            for yp in range(own // 2):
                for a in range(COMP):
                    left = []
                    for y in (2 * yp, 2 * yp + 1):
                        left.append(
                            [
                                [
                                    jnp.broadcast_to(
                                        self_f32[w * own + y : w * own + y + 1, plane(a, part, lt)],
                                        (pairs, LANE),
                                    )
                                    for part in range(2)
                                ]
                                for w in range(windows)
                            ]
                        )
                    for b in range(COMP):
                        at = ((yp * COMP + a) * COMP + b) * 2 * pairs
                        got = [product(left[y], slots[b]) for y in range(2)]
                        re = jnp.concatenate([g[0] for g in got], 0)
                        im = jnp.concatenate([g[1] for g in got], 0)
                        cross[at : at + 2 * pairs, re_at] = re.astype(jnp.bfloat16)
                        cross[at : at + 2 * pairs, im_at] = im.astype(jnp.bfloat16)
            lefts = [
                [
                    [pickx[w * stations : (w + 1) * stations, plane(a, part, lt)] for part in range(2)]
                    for w in range(windows)
                ]
                for a in range(COMP)
            ]
            for c in range(CAP):
                for b in range(COMP):
                    right = [
                        [
                            picky[
                                (c * windows + w) * stations : (c * windows + w + 1) * stations,
                                plane(b, part, lt),
                            ]
                            for part in range(2)
                        ]
                        for w in range(windows)
                    ]
                    for a in range(COMP):
                        re, im = product(lefts[a], right)
                        at = half + ((c * COMP + a) * COMP + b) * stations
                        cross[at : at + stations, re_at] = re.astype(jnp.bfloat16)
                        cross[at : at + stations, im_at] = im.astype(jnp.bfloat16)
            return carry

        lax.fori_loop(0, FREQ // LANE, one_tile, 0)
        result[...] = mm(cross[...], lag_ref[...])

        def scale_of(count):
            s = 1.0 / (jnp.maximum(count, 1.0) * math.sqrt(FREQ))
            return jnp.concatenate([s] * (LAGS // LANE), 1)

        def copies(which):
            return [
                pltpu.make_async_copy(outv.at[which, :, j], out_ref.at[:, ids[j]], sem.at[which])
                for j in range(GROUP)
            ]

        @pl.when(ch >= 2)
        def _():
            for cp in copies(slot):
                cp.wait()

        flag = lambda ref, lo, hi: ref[lo:hi, PLANE:]
        for y in range(own):
            count = None
            for w in range(windows):
                term = flag(self_f32, w * own + y, w * own + y + 1) * flag(picked, w * pairs, (w + 1) * pairs)
                count = term if count is None else count + term
            scale = scale_of(count)
            for q in range(COMP * COMP):
                at = ((y // 2) * COMP * COMP + q) * 2 * pairs + (y % 2) * pairs
                block = (result[at : at + pairs, :] * scale).astype(jnp.bfloat16)
                outv[slot, y, :, q, :, :] = block.reshape(GROUP, CAP, LAGS)
        for cp in copies(slot):
            cp.start()
        owner_row = lax.broadcasted_iota(jnp.int32, (stations, LANE), 0) // own
        for c in range(CAP):
            count = None
            for w in range(windows):
                lo = (c * windows + w) * stations
                term = flag(pickx, w * stations, (w + 1) * stations) * flag(picky, lo, lo + stations)
                count = term if count is None else count + term
            scale = scale_of(count)
            mask = []
            for y in range(own):
                m = jnp.zeros((stations, LANE), jnp.float32)
                for j in range(GROUP):
                    m = jnp.where(owner_row == j, (mine[j][c] == y).astype(jnp.float32), m)
                mask.append(m)
            for q in range(COMP * COMP):
                at = half + (c * COMP * COMP + q) * stations
                block = (result[at : at + stations, :] * scale).astype(jnp.bfloat16).astype(jnp.float32)
                square = block * block
                both = square[:, :LANE] + square[:, LANE:]
                for y in range(own):
                    acc[y * COMP * COMP + q] += both * mask[y]
        return carry

    chunks = owners // GROUP
    lax.fori_loop(0, chunks, one_chunk, 0)
    for last in range(max(chunks - 2, 0), chunks):
        for j in range(GROUP):
            pltpu.make_async_copy(
                outv.at[last % 2, :, j], out_ref.at[:, order_ref[last * GROUP + j]], sem.at[last % 2]
            ).wait()
    lane = lax.broadcasted_iota(jnp.int32, (1, LANE), 1)
    for y in range(own):
        line = jnp.zeros((1, LANE), jnp.float32)
        for q in range(COMP * COMP):
            total = jnp.sum(acc[y * COMP * COMP + q], keepdims=True).reshape(1, 1)
            line = jnp.where(lane == q, total, line)
        energy_ref[y : y + 1, :] = line[:, : COMP * COMP] / float(owners * LAGS)


def correlate(everyone, assign, target, order, own, windows):
    owners = target.shape[0]
    own_rows = own * windows
    stations, pairs = GROUP * own, GROUP * CAP
    rows = own * COMP * COMP * pairs + CAP * COMP * COMP * stations
    smem = pl.BlockSpec(memory_space=pltpu.SMEM)
    vmem = pl.BlockSpec(memory_space=pltpu.VMEM)
    f32 = jnp.float32
    return pl.pallas_call(
        functools.partial(correlate_kernel, owners, own_rows, windows),
        out_shape=(
            jax.ShapeDtypeStruct((own, owners, COMP * COMP, CAP, LAGS), jnp.bfloat16),
            jax.ShapeDtypeStruct((own, COMP * COMP), f32),
        ),
        in_specs=[smem] * 3 + [vmem] * 2,
        out_specs=(pl.BlockSpec(memory_space=pl.ANY), vmem),
        scratch_shapes=[
            pltpu.VMEM((own_rows, WIDE), f32),
            pltpu.VMEM((windows * pairs, WIDE), f32),
            pltpu.VMEM((windows * stations, WIDE), f32),
            pltpu.VMEM((CAP * windows * stations, WIDE), f32),
            pltpu.VMEM((rows, 2 * FREQ), jnp.bfloat16),
            pltpu.VMEM((rows, LAGS), f32),
            pltpu.VMEM((2, own, GROUP, COMP * COMP, CAP, LAGS), jnp.bfloat16),
            pltpu.VMEM((own * COMP * COMP, stations, LANE), f32),
            pltpu.SemaphoreType.DMA((2,)),
        ],
        compiler_params=pltpu.CompilerParams(vmem_limit_bytes=48 << 20),
        name="correlate",
    )(assign, target, order, everyone, jnp.asarray(lag_table()))


def on_device(traces, gaps, assign, target):
    own = traces.shape[0]
    windows = gaps.shape[1]
    owners = lax.axis_size("pairs")
    me = lax.axis_index("pairs")
    held = front(traces, gaps)
    masks = exchange_masks(owners)[0]
    for mask in masks:
        partner = [(i, i ^ mask) for i in range(owners)]
        held = jnp.concatenate([held, lax.ppermute(held, "pairs", partner)], 0)
    order = me ^ jnp.asarray(slot_masks(masks), jnp.int32)
    out, energy = correlate(held, assign, target, order, own, windows)
    return out.transpose(0, 1, 3, 2, 4), energy


def solution(mesh):
    in_specs = (
        P(("groups", "pairs"), None, None),
        P(("groups", "pairs"), None),
        P("groups"),
        P("groups"),
    )
    out_specs = (P(("groups", "pairs"), None, None, None, None), P(("groups", "pairs"), None))
    return jax.shard_map(
        on_device, mesh=mesh, in_specs=in_specs, out_specs=out_specs, check_vma=False
    )
```

```python
import functools
import math

import jax
import jax.numpy as jnp
import numpy as np
from jax import lax
from jax.experimental import pallas as pl
from jax.experimental.pallas import tpu as pltpu
from jax.sharding import PartitionSpec as P


SEG = 2048
FREQ = 512
FLO = 64
LAGS = 256
HALF = 21
CAP = 2
COMP = 3
RADIX = 4
LANE = 128
NONE = -1000
PART = SEG // RADIX
PLANE = 2 * COMP * FREQ
WINDOWS = 2
WIDE = WINDOWS * (PLANE + LANE)
GROUP = 4


def bin_order():
    spot = np.arange(FREQ)
    return RADIX * (spot % LANE) + spot // LANE


def dft_table():
    n1 = np.arange(PART)[:, None]
    blocks = []
    for r in (0, 2, 1, 3):
        k = FLO + RADIX * np.arange(LANE)[None, :] + r
        phase = np.mod(n1 * k, SEG) * (2.0 * math.pi / SEG)
        c, s = np.cos(phase), np.sin(phase)
        blocks.append(np.concatenate([c, -s], 1))
        if r == 1:
            blocks.append(np.concatenate([-s, -c], 1))
        if r == 3:
            blocks.append(np.concatenate([s, c], 1) * np.array([1.0]))
    return np.concatenate(blocks, 0).astype(jnp.bfloat16)


def band_table():
    f = bin_order()
    band = np.abs(f[:, None] - f[None, :]) <= HALF
    share = 1.0 / (float(COMP) * band.sum(0, keepdims=True))
    return band.astype(jnp.bfloat16), share.astype(np.float32)


def lag_table():
    bins = FLO + bin_order()[:, None]
    shifts = np.arange(LAGS)[None, :] - LAGS // 2
    phase = np.mod(bins * shifts, SEG) * (2.0 * math.pi / SEG)
    return np.concatenate([np.cos(phase), -np.sin(phase)], 0).astype(jnp.bfloat16)


def mm(a, b):
    return jnp.dot(a, b, preferred_element_type=jnp.float32)


def front_kernel(gaps_ref, x_ref, tab_ref, band_ref, share_ref, out_ref):
    windows, own = gaps_ref.shape
    rows = windows * own
    quarter = []
    for j in range(RADIX):
        per_comp = []
        for a in range(COMP):
            pieces = [
                x_ref[a, :, w * SEG + j * PART : w * SEG + (j + 1) * PART].astype(jnp.float32)
                for w in range(windows)
            ]
            per_comp.append(jnp.concatenate(pieces, 0))
        quarter.append(jnp.concatenate(per_comp, 0))
    x0, x1, x2, x3 = quarter
    even, odd = x0 + x2, x1 + x3

    def halves(y):
        low = y - y.astype(jnp.bfloat16).astype(jnp.float32)
        return jnp.concatenate([y, low], 0).astype(jnp.bfloat16)

    zero, two = halves(even + odd), halves(even - odd)
    u, v = halves(x0 - x2), halves(x1 - x3)
    tab = lambda i: tab_ref[i * PART : (i + 1) * PART, :]
    both = [
        mm(zero, tab(0)),
        mm(u, tab(2)) + mm(v, tab(3)),
        mm(two, tab(1)),
        mm(u, tab(4)) + mm(v, tab(5)),
    ]
    count = COMP * rows
    spec = [d[:count] + d[count:] for d in both]
    power = []
    for d in spec:
        total = jnp.zeros((rows, LANE), jnp.float32)
        for a in range(COMP):
            re = d[a * rows : (a + 1) * rows, :LANE]
            im = d[a * rows : (a + 1) * rows, LANE:]
            total = total + (re * re + im * im)
        power.append(total)
    power = jnp.concatenate(power, 1)
    p1 = power.astype(jnp.bfloat16).astype(jnp.float32)
    rest = power - p1
    p2 = rest.astype(jnp.bfloat16).astype(jnp.float32)
    p3 = rest - p2
    sums = mm(jnp.concatenate([p1, p2, p3], 0).astype(jnp.bfloat16), band_ref[...])
    smooth = (sums[:rows] + sums[rows : 2 * rows] + sums[2 * rows :]) * share_ref[...]
    row_at = lax.broadcasted_iota(jnp.int32, (rows, LANE), 0)
    flags = jnp.zeros((rows, LANE), jnp.float32)
    for w in range(windows):
        for s in range(own):
            flags = jnp.where(row_at == w * own + s, gaps_ref[w, s].astype(jnp.float32), flags)
    wide_flags = jnp.concatenate([flags] * RADIX, 1)
    factor = wide_flags / jnp.sqrt(smooth + 1e-06)
    for a in range(COMP):
        for part in range(2):
            whole = jnp.concatenate(
                [d[a * rows : (a + 1) * rows, part * LANE : (part + 1) * LANE] for d in spec], 1
            )
            white = whole * factor
            for w in range(windows):
                start = w * PLANE + (2 * a + part) * FREQ
                out_ref[:, start : start + FREQ] = white[w * own : (w + 1) * own].astype(jnp.bfloat16)
    for w in range(windows):
        start = windows * PLANE + w * LANE
        out_ref[:, start : start + LANE] = flags[w * own : (w + 1) * own].astype(jnp.bfloat16)


def front(traces, gaps):
    own, comps, length = traces.shape
    windows = gaps.shape[1]
    assert comps == COMP and length == windows * SEG
    band, share = band_table()
    vmem = pl.BlockSpec(memory_space=pltpu.VMEM)
    return pl.pallas_call(
        front_kernel,
        out_shape=jax.ShapeDtypeStruct((own, windows * (PLANE + LANE)), jnp.bfloat16),
        in_specs=[pl.BlockSpec(memory_space=pltpu.SMEM)] + [vmem] * 4,
        out_specs=vmem,
        compiler_params=room(0),
        name="front",
    )(
        gaps.T,
        traces.transpose(1, 0, 2),
        jnp.asarray(dft_table()),
        jnp.asarray(band),
        jnp.asarray(share),
    )


def exchange_plan(count):
    bits = int(count).bit_length() - 1
    assert count == 1 << bits and bits >= 3
    chips = [1 << b for b in range(bits - 1, 0, -1)]
    return [chips, chips[-1:] + chips[:-1]]


def owner_masks(plan):
    own_core = []
    for chips in plan:
        found = [0]
        for m in chips:
            found = found + [f ^ m for f in found]
        own_core.append(found)
    return np.asarray(
        [own_core[p] + [1 ^ f for f in own_core[1 - p]] for p in range(2)], np.int32
    )


def room(operand_bytes):
    return pltpu.CompilerParams(vmem_limit_bytes=(8 << 20) + operand_bytes)


def first_two(flags):
    found = [jnp.int32(NONE)] * CAP
    seen = jnp.int32(0)
    for s, flag in enumerate(flags):
        for c in range(CAP):
            found[c] = jnp.where(jnp.logical_and(flag, seen == c), s, found[c])
        seen = seen + flag.astype(jnp.int32)
    return found


def iota(rows, cols, dim):
    return lax.broadcasted_iota(jnp.int32, (rows, cols), dim)


def one_hot(want, cols):
    return jnp.where(iota(want.shape[0], cols, 1) == want, 1.0, 0.0).astype(jnp.bfloat16)


def own_slots(assign_ref, target_ref, me, own, owner):
    want = target_ref[owner]
    return first_two([assign_ref[me * own + s] == want for s in range(own)])


def spread_kernel(own, assign_ref, target_ref, mask_ref, self_ref, rows_ref, partner_ref):
    me = lax.axis_index("pairs")
    parity = lax.rem(me, 2)
    pairs = GROUP * CAP
    stations = GROUP * own
    mine_rows = self_ref[...]
    rows_ref[...] = mm(one_hot(iota(own * pairs, own, 0) // pairs, own), mine_rows).astype(
        jnp.bfloat16
    )
    place = iota(CAP * stations, own, 0)
    place = (place // stations) * GROUP + (place % stations) // own

    def one_chunk(ch, carry):
        want = jnp.full(place.shape, NONE, jnp.int32)
        for j in range(GROUP):
            owner = me ^ mask_ref[parity, ch * GROUP + j]
            for c, s in enumerate(own_slots(assign_ref, target_ref, me, own, owner)):
                want = jnp.where(place == c * GROUP + j, s, want)
        partner_ref[ch] = mm(one_hot(want, own), mine_rows).astype(jnp.bfloat16)
        return carry

    lax.fori_loop(0, partner_ref.shape[0], one_chunk, 0)


def spread(held, assign, target, masks):
    own = held.shape[0]
    chunks = masks.shape[1] // GROUP
    smem = pl.BlockSpec(memory_space=pltpu.SMEM)
    vmem = pl.BlockSpec(memory_space=pltpu.VMEM)
    made = own * GROUP * CAP + chunks * CAP * GROUP * own
    return pl.pallas_call(
        functools.partial(spread_kernel, own),
        out_shape=(
            jax.ShapeDtypeStruct((own * GROUP * CAP, WIDE), jnp.bfloat16),
            jax.ShapeDtypeStruct((chunks, CAP * GROUP * own, WIDE), jnp.bfloat16),
        ),
        in_specs=[smem] * 3 + [vmem],
        out_specs=(vmem, vmem),
        compiler_params=room(2 * made * WIDE),
        cost_estimate=pl.CostEstimate(
            flops=2 * made * own * WIDE, bytes_accessed=2 * made * WIDE, transcendentals=0
        ),
        name="spread",
    )(assign, target, masks, held)


def correlate_kernel(
    owners, own, windows, base, first, last, assign_ref, target_ref, mask_ref, chunk_ref, rows_ref,
    partner_ref, lag_ref, *rest,
):
    if not first:
        sum_in, rest = rest[0], rest[2:]
    out_ref, sum_ref, picked, cross, result, outv, sem = rest
    me = lax.axis_index("pairs")
    parity = lax.rem(me, 2)
    pairs = GROUP * CAP
    stations = GROUP * own
    nine = COMP * COMP
    half = own * nine * pairs
    chunks = chunk_ref.shape[0] // stations
    my_target = target_ref[me]
    total = jnp.zeros((own, nine * LANE), jnp.float32) if first else sum_in[...]

    def owner_of(ch, j):
        return me ^ mask_ref[parity, base + ch * GROUP + j]

    def copies(ch):
        which = lax.rem(ch, 2)
        return [
            pltpu.make_async_copy(outv.at[which, :, j], out_ref.at[:, owner_of(ch, j)], sem.at[which])
            for j in range(GROUP)
        ]

    def one_chunk(ch, total):
        slot = lax.rem(ch, 2)
        first_row = ch * stations if isinstance(ch, int) else pl.multiple_of(ch * stations, stations)
        here = pl.ds(first_row, stations)
        row = iota(2 * pairs, stations, 0) % pairs
        want = jnp.full(row.shape, NONE, jnp.int32)
        mine = []
        for j in range(GROUP):
            owner = owner_of(ch, j)
            theirs = first_two([assign_ref[owner * own + s] == my_target for s in range(own)])
            for c, s in enumerate(theirs):
                want = jnp.where(row == j * CAP + c, s + j * own, want)
            mine.append(own_slots(assign_ref, target_ref, me, own, owner))
        picked[...] = mm(one_hot(want, stations), chunk_ref[here, :]).astype(jnp.bfloat16)

        def product(left, right):
            re = im = None
            for (lr, li), (rr, ri) in zip(left, right):
                r = lr * rr + li * ri
                i = li * rr - lr * ri
                re = r if re is None else re + r
                im = i if im is None else im + i
            return re, im

        def one_tile(lt, carry):
            re_at = pl.ds(pl.multiple_of(lt * LANE, LANE), LANE)
            im_at = pl.ds(pl.multiple_of(FREQ + lt * LANE, LANE), LANE)

            def tile(load, a):
                got = []
                for w in range(windows):
                    both = []
                    for part in range(2):
                        start = ((w * COMP + a) * 2 + part) * FREQ + lt * LANE
                        both.append(load(pl.ds(pl.multiple_of(start, LANE), LANE)))
                    got.append(both)
                return got

            slots = [tile(lambda d: picked[:, d], b) for b in range(COMP)]
            for yp in range(own // 2):
                for a in range(COMP):
                    left = tile(lambda d: rows_ref[yp * 2 * pairs : (yp + 1) * 2 * pairs, d], a)
                    for b in range(COMP):
                        at = ((yp * COMP + a) * COMP + b) * 2 * pairs
                        re, im = product(left, slots[b])
                        cross[at : at + 2 * pairs, re_at] = re
                        cross[at : at + 2 * pairs, im_at] = im
            lefts = [tile(lambda d: chunk_ref[here, d], a) for a in range(COMP)]
            for c in range(CAP):
                for b in range(COMP):
                    right = tile(
                        lambda d: partner_ref[base // GROUP + ch, c * stations : (c + 1) * stations, d], b
                    )
                    for a in range(COMP):
                        re, im = product(lefts[a], right)
                        at = half + ((c * COMP + a) * COMP + b) * stations
                        cross[at : at + stations, re_at] = re
                        cross[at : at + stations, im_at] = im
            return carry

        lax.fori_loop(0, FREQ // LANE, one_tile, 0)
        result[...] = mm(cross[...], lag_ref[...])

        def flag(ref, rows, w):
            return ref[rows, PLANE * windows + w * LANE : PLANE * windows + (w + 1) * LANE]

        if not isinstance(ch, int):

            @pl.when(ch >= 2)
            def _():
                for cp in copies(ch):
                    cp.wait()

        for yp in range(own // 2):
            count = None
            for w in range(windows):
                left = flag(rows_ref, slice(yp * 2 * pairs, (yp + 1) * 2 * pairs), w)
                term = left.astype(jnp.float32) * flag(picked, slice(None), w).astype(jnp.float32)
                count = term if count is None else count + term
            scale = 1.0 / (jnp.maximum(count, 1.0) * math.sqrt(FREQ))
            scale = jnp.concatenate([scale] * (LAGS // LANE), 1)
            for q in range(nine):
                at = (yp * nine + q) * 2 * pairs
                block = (result[at : at + 2 * pairs, :] * scale).astype(jnp.bfloat16)
                outv[slot, 2 * yp : 2 * yp + 2, :, q, :, :] = block.reshape(2, GROUP, CAP, LAGS)
        for cp in copies(ch):
            cp.start()
        weights, squares = [], []
        col = iota(own, stations, 1) // own
        y_row = iota(own, stations, 0)
        for c in range(CAP):
            weight = jnp.zeros((own, stations), jnp.float32)
            for j in range(GROUP):
                hit = jnp.logical_and(col == j, y_row == mine[j][c])
                weight = jnp.where(hit, 1.0, weight)
            weights.append(weight)
            count = None
            for w in range(windows):
                left = flag(chunk_ref, here, w).astype(jnp.float32)
                part_rows = slice(c * stations, (c + 1) * stations)
                lanes = slice(PLANE * windows + w * LANE, PLANE * windows + (w + 1) * LANE)
                right = partner_ref[base // GROUP + ch, part_rows, lanes].astype(jnp.float32)
                term = left * right
                count = term if count is None else count + term
            most = jnp.maximum(count, 1.0)
            share = 1.0 / (most * most * float(FREQ))
            tiles = []
            for q in range(nine):
                at = half + (c * nine + q) * stations
                block = result[at : at + stations, :]
                square = block * block
                both = square[:, :LANE]
                for lt in range(1, LAGS // LANE):
                    both = both + square[:, lt * LANE : (lt + 1) * LANE]
                tiles.append(both * share)
            squares.append(jnp.concatenate(tiles, 1))
        weights = jnp.concatenate(weights, 1).astype(jnp.bfloat16)
        return total + mm(weights, jnp.concatenate(squares, 0).astype(jnp.bfloat16))

    if chunks == 1:
        total = one_chunk(0, total)
    else:
        total = lax.fori_loop(0, chunks, one_chunk, total)
    if last:
        lane = iota(own, nine, 1)
        energy = jnp.zeros((own, nine), jnp.float32)
        for q in range(nine):
            part = jnp.sum(total[:, q * LANE : (q + 1) * LANE], axis=1, keepdims=True)
            energy = jnp.where(lane == q, part, energy)
        sum_ref[...] = energy / float(owners * LAGS)
    else:
        sum_ref[...] = total
    for ch in range(max(chunks - 2, 0), chunks):
        for cp in copies(ch):
            cp.wait()


def correlate(chunk, base, spreads, carried, last, assign, target, masks, lags):
    rows, partners = spreads
    owners = target.shape[0]
    own = assign.shape[0] // owners
    windows = (rows.shape[1] - 0) // (PLANE + LANE)
    nine = COMP * COMP
    stations, pairs = GROUP * own, GROUP * CAP
    lines = own * nine * pairs + CAP * nine * stations
    smem = pl.BlockSpec(memory_space=pltpu.SMEM)
    vmem = pl.BlockSpec(memory_space=pltpu.VMEM)
    anywhere = pl.BlockSpec(memory_space=pl.ANY)
    f32, bf16 = jnp.float32, jnp.bfloat16
    first = carried is None
    operands = [assign, target, masks, chunk, rows, partners, lags]
    specs = [smem] * 3 + [vmem] * 4
    aliases = {}
    if not first:
        out_so_far, sums = carried
        operands += [sums, out_so_far]
        specs += [vmem, anywhere]
        aliases = {len(operands) - 1: 0}
    sum_shape = (own, nine) if last else (own, nine * LANE)
    chunks = chunk.shape[0] // stations
    return pl.pallas_call(
        functools.partial(correlate_kernel, owners, own, windows, base, first, last),
        out_shape=(
            jax.ShapeDtypeStruct((own, owners, nine, CAP, LAGS), bf16),
            jax.ShapeDtypeStruct(sum_shape, f32),
        ),
        in_specs=specs,
        out_specs=(anywhere, vmem),
        input_output_aliases=aliases,
        scratch_shapes=[
            pltpu.VMEM((2 * pairs, WIDE), bf16),
            pltpu.VMEM((lines, 2 * FREQ), bf16),
            pltpu.VMEM((lines, LAGS), f32),
            pltpu.VMEM((2, own, GROUP, nine, CAP, LAGS), bf16),
            pltpu.SemaphoreType.DMA((2,)),
        ],
        compiler_params=room(2 * (chunk.size + rows.size + partners.size)),
        cost_estimate=pl.CostEstimate(
            flops=chunks * 4 * lines * FREQ * LAGS,
            bytes_accessed=chunks * 2 * lines * LAGS,
            transcendentals=0,
        ),
        name="correlate",
    )(*operands)


def steps_of(traces, gaps, assign, target):
    owners = lax.axis_size("pairs")
    plan = exchange_plan(owners)
    masks = jnp.asarray(owner_masks(plan))
    lags = jnp.asarray(lag_table())

    def swap(block, masks_of):
        return lax.ppermute(block, "pairs", [(i, i ^ masks_of[i % 2]) for i in range(owners)])

    steps = [tuple(m) for m in zip(*plan)]
    held = front(traces, gaps)
    spreads = spread(held, assign, target, masks)
    for step in steps[:2]:
        got = swap(held, step)
        held = jnp.concatenate([held, got], 0)
    blocks = [held]
    for step in steps[2:]:
        sent = jnp.concatenate(blocks, 0) if len(blocks) > 1 else held
        blocks.append(swap(sent, step))
    other = []
    for block in blocks:
        other.append(swap(block, (1, 1)))
    base = 0
    order = []
    for block in blocks + other:
        order.append((block, base))
        base += block.shape[0] // traces.shape[0]
    count = len(blocks)
    ranked = [order[i + side * count] for i in range(count) for side in range(2)]
    carried = None
    for at, (block, start) in enumerate(ranked):
        last = at == len(ranked) - 1
        carried = correlate(block, start, spreads, carried, last, assign, target, masks, lags)
    out, energy = carried
    return out.transpose(0, 1, 3, 2, 4), energy


def solution(mesh):
    in_specs = (
        P(("groups", "pairs"), None, None),
        P(("groups", "pairs"), None),
        P("groups"),
        P("groups"),
    )
    out_specs = (P(("groups", "pairs"), None, None, None, None), P(("groups", "pairs"), None))
    return jax.shard_map(
        steps_of, mesh=mesh, in_specs=in_specs, out_specs=out_specs, check_vma=False
    )
```

```python
import functools
import math

import jax
import jax.numpy as jnp
import numpy as np
from jax import lax
from jax.experimental import pallas as pl
from jax.experimental.pallas import tpu as pltpu
from jax.sharding import PartitionSpec as P


SEG = 2048
FREQ = 512
FLO = 64
LAGS = 256
HALF = 21
CAP = 2
COMP = 3
RADIX = 4
LANE = 128
TILE = 2 * LANE
NONE = -1000
PART = SEG // RADIX
PLANE = 2 * COMP * FREQ
WINDOWS = 2
WIDE = WINDOWS * (PLANE + LANE)
GROUP = 4


def bin_order():
    spot = np.arange(FREQ)
    return RADIX * (spot % LANE) + spot // LANE


def dft_table():
    n1 = np.arange(PART)[:, None]
    blocks = []
    for r in (0, 2, 1, 3):
        k = FLO + RADIX * np.arange(LANE)[None, :] + r
        phase = np.mod(n1 * k, SEG) * (2.0 * math.pi / SEG)
        c, s = np.cos(phase), np.sin(phase)
        blocks.append(np.concatenate([c, -s], 1))
        if r == 1:
            blocks.append(np.concatenate([-s, -c], 1))
        if r == 3:
            blocks.append(np.concatenate([s, c], 1) * np.array([1.0]))
    return np.concatenate(blocks, 0).astype(jnp.bfloat16)


def band_table():
    f = bin_order()
    return (np.abs(f[:, None] - f[None, :]) <= HALF).astype(jnp.bfloat16)


def lag_table():
    bins = FLO + bin_order()[:, None]
    shifts = np.arange(LAGS)[None, :] - LAGS // 2
    phase = np.mod(bins * shifts, SEG) * (2.0 * math.pi / SEG)
    return np.concatenate([np.cos(phase), -np.sin(phase)], 0).astype(jnp.bfloat16)


def mm(a, b):
    return jnp.dot(a, b, preferred_element_type=jnp.float32)


def front_kernel(gaps_hbm, x_hbm, tab_hbm, band_hbm, out_ref, gaps_ref, x_ref, tab_ref, band_ref, sem):
    windows, own = gaps_ref.shape
    rows = windows * own
    parts = tab_ref.shape[0] // PART

    def part_at(i):
        return pl.ds(i * PART, PART)

    loads = [
        pltpu.make_async_copy(x_hbm, x_ref, sem.at[0]),
        *[
            pltpu.make_async_copy(tab_hbm.at[part_at(i)], tab_ref.at[part_at(i)], sem.at[1 + i])
            for i in range(parts)
        ],
        pltpu.make_async_copy(band_hbm, band_ref, sem.at[1 + parts]),
        pltpu.make_async_copy(gaps_hbm, gaps_ref, sem.at[2 + parts]),
    ]
    for load in loads:
        load.start()
    loads[0].wait()
    quarter = []
    for j in range(RADIX):
        per_comp = []
        for a in range(COMP):
            pieces = [
                x_ref[a, :, w * SEG + j * PART : w * SEG + (j + 1) * PART].astype(jnp.float32)
                for w in range(windows)
            ]
            per_comp.append(jnp.concatenate(pieces, 0))
        quarter.append(jnp.concatenate(per_comp, 0))
    x0, x1, x2, x3 = quarter
    even, odd = x0 + x2, x1 + x3

    def halves(y):
        low = y - y.astype(jnp.bfloat16).astype(jnp.float32)
        return jnp.concatenate([y, low], 0).astype(jnp.bfloat16)

    zero, two = halves(even + odd), halves(even - odd)
    u, v = halves(x0 - x2), halves(x1 - x3)

    def tab(i):
        loads[1 + i].wait()
        return tab_ref[part_at(i), :]

    both0 = mm(zero, tab(0))
    both2 = mm(two, tab(1))
    both1 = mm(u, tab(2)) + mm(v, tab(3))
    both3 = mm(u, tab(4)) + mm(v, tab(5))
    both = [both0, both1, both2, both3]
    count = COMP * rows
    spec = [d[:count] + d[count:] for d in both]
    power = []
    for d in spec:
        total = jnp.zeros((rows, LANE), jnp.float32)
        for a in range(COMP):
            re = d[a * rows : (a + 1) * rows, :LANE]
            im = d[a * rows : (a + 1) * rows, LANE:]
            total = total + (re * re + im * im)
        power.append(total)
    power = jnp.concatenate(power, 1)
    p1 = power.astype(jnp.bfloat16).astype(jnp.float32)
    rest = power - p1
    p2 = rest.astype(jnp.bfloat16).astype(jnp.float32)
    p3 = rest - p2
    loads[1 + parts].wait()
    sums = mm(jnp.concatenate([p1, p2, p3], 0).astype(jnp.bfloat16), band_ref[...])
    spot = iota(rows, FREQ, 1)
    f = RADIX * (spot % LANE) + spot // LANE
    taken = jnp.minimum(f + HALF, FREQ - 1) - jnp.maximum(f - HALF, 0) + 1
    share = 1.0 / (taken.astype(jnp.float32) * float(COMP))
    smooth = (sums[:rows] + sums[rows : 2 * rows] + sums[2 * rows :]) * share
    loads[2 + parts].wait()
    row_at = lax.broadcasted_iota(jnp.int32, (rows, LANE), 0)
    flags = jnp.zeros((rows, LANE), jnp.float32)
    for w in range(windows):
        for s in range(own):
            flags = jnp.where(row_at == w * own + s, gaps_ref[w, s].astype(jnp.float32), flags)
    wide_flags = jnp.concatenate([flags] * RADIX, 1)
    factor = wide_flags / jnp.sqrt(smooth + 1e-06)
    for a in range(COMP):
        for part in range(2):
            whole = jnp.concatenate(
                [d[a * rows : (a + 1) * rows, part * LANE : (part + 1) * LANE] for d in spec], 1
            )
            white = whole * factor
            for w in range(windows):
                start = w * PLANE + (2 * a + part) * FREQ
                out_ref[:, start : start + FREQ] = white[w * own : (w + 1) * own].astype(jnp.bfloat16)
    for w in range(windows):
        start = windows * PLANE + w * LANE
        out_ref[:, start : start + LANE] = flags[w * own : (w + 1) * own].astype(jnp.bfloat16)


def front(traces, gaps):
    own, comps, length = traces.shape
    windows = gaps.shape[1]
    assert comps == COMP and length == windows * SEG
    table, band = dft_table(), band_table()
    operands = (gaps.T, traces.transpose(1, 0, 2), jnp.asarray(table), jnp.asarray(band))
    hbm = pl.BlockSpec(memory_space=pltpu.HBM)
    bf16 = jnp.bfloat16
    return pl.pallas_call(
        front_kernel,
        out_shape=jax.ShapeDtypeStruct((own, windows * (PLANE + LANE)), bf16),
        in_specs=[hbm] * 4,
        out_specs=pl.BlockSpec(memory_space=pltpu.VMEM),
        scratch_shapes=[
            pltpu.SMEM((windows, own), jnp.int32),
            pltpu.VMEM((comps, own, length), bf16),
            pltpu.VMEM(table.shape, bf16),
            pltpu.VMEM(band.shape, bf16),
            pltpu.SemaphoreType.DMA((3 + table.shape[0] // PART,)),
        ],
        compiler_params=room(0),
        name="front",
    )(*[pltpu.with_memory_space_constraint(v, pltpu.HBM) for v in operands])


def exchange_plan(count):
    bits = int(count).bit_length() - 1
    assert count == 1 << bits and bits >= 3
    chips = [1 << b for b in range(bits - 1, 0, -1)]
    return [chips, chips[-1:] + chips[:-1]]


def owner_masks(plan):
    own_core = []
    for chips in plan:
        found = [0]
        for m in chips:
            found = found + [f ^ m for f in found]
        own_core.append(found)
    return np.asarray(
        [own_core[p] + [1 ^ f for f in own_core[1 - p]] for p in range(2)], np.int32
    )


def room(operand_bytes):
    return pltpu.CompilerParams(vmem_limit_bytes=(8 << 20) + operand_bytes)


def first_two(flags):
    found = [jnp.int32(NONE)] * CAP
    seen = jnp.int32(0)
    for s, flag in enumerate(flags):
        for c in range(CAP):
            found[c] = jnp.where(jnp.logical_and(flag, seen == c), s, found[c])
        seen = seen + flag.astype(jnp.int32)
    return found


def iota(rows, cols, dim):
    return lax.broadcasted_iota(jnp.int32, (rows, cols), dim)


def one_hot(want, cols):
    return jnp.where(iota(want.shape[0], cols, 1) == want, 1.0, 0.0).astype(jnp.bfloat16)


def own_slots(assign_ref, target_ref, me, own, owner):
    want = target_ref[owner]
    return first_two([assign_ref[me * own + s] == want for s in range(own)])


def spread_kernel(own, assign_ref, target_ref, mask_ref, self_ref, rows_ref, partner_ref):
    me = lax.axis_index("pairs")
    parity = lax.rem(me, 2)
    pairs = GROUP * CAP
    stations = GROUP * own
    mine_rows = self_ref[...]
    rows_ref[...] = mm(one_hot(iota(own * pairs, own, 0) // pairs, own), mine_rows).astype(
        jnp.bfloat16
    )
    place = iota(CAP * stations, own, 0)
    place = (place // stations) * GROUP + (place % stations) // own

    def one_chunk(ch, carry):
        want = jnp.full(place.shape, NONE, jnp.int32)
        for j in range(GROUP):
            owner = me ^ mask_ref[parity, ch * GROUP + j]
            for c, s in enumerate(own_slots(assign_ref, target_ref, me, own, owner)):
                want = jnp.where(place == c * GROUP + j, s, want)
        partner_ref[ch] = mm(one_hot(want, own), mine_rows).astype(jnp.bfloat16)
        return carry

    lax.fori_loop(0, partner_ref.shape[0], one_chunk, 0)


def spread(held, assign, target, masks):
    own = held.shape[0]
    chunks = masks.shape[1] // GROUP
    smem = pl.BlockSpec(memory_space=pltpu.SMEM)
    vmem = pl.BlockSpec(memory_space=pltpu.VMEM)
    made = own * GROUP * CAP + chunks * CAP * GROUP * own
    return pl.pallas_call(
        functools.partial(spread_kernel, own),
        out_shape=(
            jax.ShapeDtypeStruct((own * GROUP * CAP, WIDE), jnp.bfloat16),
            jax.ShapeDtypeStruct((chunks, CAP * GROUP * own, WIDE), jnp.bfloat16),
        ),
        in_specs=[smem] * 3 + [vmem],
        out_specs=(vmem, vmem),
        compiler_params=room(2 * made * WIDE),
        cost_estimate=pl.CostEstimate(
            flops=2 * made * own * WIDE, bytes_accessed=2 * made * WIDE, transcendentals=0
        ),
        name="spread",
    )(assign, target, masks, held)


def correlate_kernel(
    owners, own, windows, base, first, last, assign_ref, target_ref, mask_ref, chunk_ref, rows_ref,
    partner_ref, lag_ref, *rest,
):
    if not first:
        sum_in, rest = rest[0], rest[2:]
    out_ref, sum_ref, picked, cross, result, outv, sem = rest
    me = lax.axis_index("pairs")
    parity = lax.rem(me, 2)
    pairs = GROUP * CAP
    stations = GROUP * own
    nine = COMP * COMP
    half = own * nine * pairs
    chunks = chunk_ref.shape[0] // stations
    my_target = target_ref[me]
    total = jnp.zeros((own, nine * LANE), jnp.float32) if first else sum_in[...]

    def owner_of(ch, j):
        return me ^ mask_ref[parity, base + ch * GROUP + j]

    def copies(ch):
        which = lax.rem(ch, 2)
        return [
            pltpu.make_async_copy(outv.at[which, :, j], out_ref.at[:, owner_of(ch, j)], sem.at[which])
            for j in range(GROUP)
        ]

    def one_chunk(ch, total):
        slot = lax.rem(ch, 2)
        first_row = ch * stations if isinstance(ch, int) else pl.multiple_of(ch * stations, stations)
        here = pl.ds(first_row, stations)
        row = iota(2 * pairs, stations, 0) % pairs
        want = jnp.full(row.shape, NONE, jnp.int32)
        mine = []
        for j in range(GROUP):
            owner = owner_of(ch, j)
            theirs = first_two([assign_ref[owner * own + s] == my_target for s in range(own)])
            for c, s in enumerate(theirs):
                want = jnp.where(row == j * CAP + c, s + j * own, want)
            mine.append(own_slots(assign_ref, target_ref, me, own, owner))
        picked[...] = mm(one_hot(want, stations), chunk_ref[here, :]).astype(jnp.bfloat16)

        def product(left, right):
            re = im = None
            for (lr, li), (rr, ri) in zip(left, right):
                r = lr * rr + li * ri
                i = li * rr - lr * ri
                re = r if re is None else re + r
                im = i if im is None else im + i
            return re, im

        def one_tile(lt, carry):
            re_at = pl.ds(pl.multiple_of(lt * TILE, TILE), TILE)
            im_at = pl.ds(pl.multiple_of(FREQ + lt * TILE, TILE), TILE)

            def tile(load, a):
                got = []
                for w in range(windows):
                    both = []
                    for part in range(2):
                        start = ((w * COMP + a) * 2 + part) * FREQ + lt * TILE
                        both.append(load(pl.ds(pl.multiple_of(start, TILE), TILE)))
                    got.append(both)
                return got

            slots = [tile(lambda d: picked[:, d], b) for b in range(COMP)]
            for yp in range(own // 2):
                for a in range(COMP):
                    left = tile(lambda d: rows_ref[yp * 2 * pairs : (yp + 1) * 2 * pairs, d], a)
                    for b in range(COMP):
                        at = ((yp * COMP + a) * COMP + b) * 2 * pairs
                        re, im = product(left, slots[b])
                        cross[at : at + 2 * pairs, re_at] = re
                        cross[at : at + 2 * pairs, im_at] = im
            lefts = [tile(lambda d: chunk_ref[here, d], a) for a in range(COMP)]
            for c in range(CAP):
                for b in range(COMP):
                    right = tile(
                        lambda d: partner_ref[base // GROUP + ch, c * stations : (c + 1) * stations, d], b
                    )
                    for a in range(COMP):
                        re, im = product(lefts[a], right)
                        at = half + ((c * COMP + a) * COMP + b) * stations
                        cross[at : at + stations, re_at] = re
                        cross[at : at + stations, im_at] = im
            return carry

        lax.fori_loop(0, FREQ // TILE, one_tile, 0)
        result[...] = mm(cross[...], lag_ref[...])

        def flag(ref, rows, w):
            return ref[rows, PLANE * windows + w * LANE : PLANE * windows + (w + 1) * LANE]

        if not isinstance(ch, int):

            @pl.when(ch >= 2)
            def _():
                for cp in copies(ch):
                    cp.wait()

        for yp in range(own // 2):
            count = None
            for w in range(windows):
                left = flag(rows_ref, slice(yp * 2 * pairs, (yp + 1) * 2 * pairs), w)
                term = left.astype(jnp.float32) * flag(picked, slice(None), w).astype(jnp.float32)
                count = term if count is None else count + term
            scale = 1.0 / (jnp.maximum(count, 1.0) * math.sqrt(FREQ))
            scale = jnp.concatenate([scale] * (LAGS // LANE), 1)
            for q in range(nine):
                at = (yp * nine + q) * 2 * pairs
                block = (result[at : at + 2 * pairs, :] * scale).astype(jnp.bfloat16)
                outv[slot, 2 * yp : 2 * yp + 2, :, q, :, :] = block.reshape(2, GROUP, CAP, LAGS)
        for cp in copies(ch):
            cp.start()
        weights, squares = [], []
        col = iota(own, stations, 1) // own
        y_row = iota(own, stations, 0)
        for c in range(CAP):
            weight = jnp.zeros((own, stations), jnp.float32)
            for j in range(GROUP):
                hit = jnp.logical_and(col == j, y_row == mine[j][c])
                weight = jnp.where(hit, 1.0, weight)
            weights.append(weight)
            count = None
            for w in range(windows):
                left = flag(chunk_ref, here, w).astype(jnp.float32)
                part_rows = slice(c * stations, (c + 1) * stations)
                lanes = slice(PLANE * windows + w * LANE, PLANE * windows + (w + 1) * LANE)
                right = partner_ref[base // GROUP + ch, part_rows, lanes].astype(jnp.float32)
                term = left * right
                count = term if count is None else count + term
            most = jnp.maximum(count, 1.0)
            share = 1.0 / (most * most * float(FREQ))
            tiles = []
            for q in range(nine):
                at = half + (c * nine + q) * stations
                block = result[at : at + stations, :]
                square = block * block
                both = square[:, :LANE]
                for lt in range(1, LAGS // LANE):
                    both = both + square[:, lt * LANE : (lt + 1) * LANE]
                tiles.append(both * share)
            squares.append(jnp.concatenate(tiles, 1))
        weights = jnp.concatenate(weights, 1).astype(jnp.bfloat16)
        return total + mm(weights, jnp.concatenate(squares, 0).astype(jnp.bfloat16))

    if chunks == 1:
        total = one_chunk(0, total)
    else:
        total = lax.fori_loop(0, chunks, one_chunk, total)
    if last:
        lane = iota(own, nine, 1)
        energy = jnp.zeros((own, nine), jnp.float32)
        for q in range(nine):
            part = jnp.sum(total[:, q * LANE : (q + 1) * LANE], axis=1, keepdims=True)
            energy = jnp.where(lane == q, part, energy)
        sum_ref[...] = energy / float(owners * LAGS)
    else:
        sum_ref[...] = total
    for ch in range(max(chunks - 2, 0), chunks):
        for cp in copies(ch):
            cp.wait()


def correlate(chunk, base, spreads, carried, last, assign, target, masks, lags):
    rows, partners = spreads
    owners = target.shape[0]
    own = assign.shape[0] // owners
    windows = (rows.shape[1] - 0) // (PLANE + LANE)
    nine = COMP * COMP
    stations, pairs = GROUP * own, GROUP * CAP
    lines = own * nine * pairs + CAP * nine * stations
    smem = pl.BlockSpec(memory_space=pltpu.SMEM)
    vmem = pl.BlockSpec(memory_space=pltpu.VMEM)
    anywhere = pl.BlockSpec(memory_space=pl.ANY)
    f32, bf16 = jnp.float32, jnp.bfloat16
    first = carried is None
    operands = [assign, target, masks, chunk, rows, partners, lags]
    specs = [smem] * 3 + [vmem] * 4
    aliases = {}
    if not first:
        out_so_far, sums = carried
        operands += [sums, out_so_far]
        specs += [vmem, anywhere]
        aliases = {len(operands) - 1: 0}
    sum_shape = (own, nine) if last else (own, nine * LANE)
    chunks = chunk.shape[0] // stations
    return pl.pallas_call(
        functools.partial(correlate_kernel, owners, own, windows, base, first, last),
        out_shape=(
            jax.ShapeDtypeStruct((own, owners, nine, CAP, LAGS), bf16),
            jax.ShapeDtypeStruct(sum_shape, f32),
        ),
        in_specs=specs,
        out_specs=(anywhere, vmem),
        input_output_aliases=aliases,
        scratch_shapes=[
            pltpu.VMEM((2 * pairs, WIDE), bf16),
            pltpu.VMEM((lines, 2 * FREQ), bf16),
            pltpu.VMEM((lines, LAGS), f32),
            pltpu.VMEM((2, own, GROUP, nine, CAP, LAGS), bf16),
            pltpu.SemaphoreType.DMA((2,)),
        ],
        compiler_params=room(2 * (chunk.size + rows.size + partners.size)),
        cost_estimate=pl.CostEstimate(
            flops=chunks * 4 * lines * FREQ * LAGS,
            bytes_accessed=chunks * 2 * lines * LAGS,
            transcendentals=0,
        ),
        name="correlate",
    )(*operands)


def steps_of(traces, gaps, assign, target):
    owners = lax.axis_size("pairs")
    plan = exchange_plan(owners)
    masks = jnp.asarray(owner_masks(plan))
    lags = jnp.asarray(lag_table())

    def swap(block, masks_of):
        return lax.ppermute(block, "pairs", [(i, i ^ masks_of[i % 2]) for i in range(owners)])

    steps = [tuple(m) for m in zip(*plan)]
    held = front(traces, gaps)
    spreads = spread(held, assign, target, masks)
    for step in steps[:2]:
        got = swap(held, step)
        held = jnp.concatenate([held, got], 0)
    blocks = [held]
    for step in steps[2:]:
        sent = jnp.concatenate(blocks, 0) if len(blocks) > 1 else held
        blocks.append(swap(sent, step))
    other = []
    for block in blocks:
        other.append(swap(block, (1, 1)))
    base = 0
    order = []
    for block in blocks + other:
        order.append((block, base))
        base += block.shape[0] // traces.shape[0]
    count = len(blocks)
    ranked = [order[i + side * count] for i in range(count) for side in range(2)]
    carried = None
    for at, (block, start) in enumerate(ranked):
        last = at == len(ranked) - 1
        carried = correlate(block, start, spreads, carried, last, assign, target, masks, lags)
    out, energy = carried
    return out.transpose(0, 1, 3, 2, 4), energy


def solution(mesh):
    in_specs = (
        P(("groups", "pairs"), None, None),
        P(("groups", "pairs"), None),
        P("groups"),
        P("groups"),
    )
    out_specs = (P(("groups", "pairs"), None, None, None, None), P(("groups", "pairs"), None))
    return jax.shard_map(
        steps_of, mesh=mesh, in_specs=in_specs, out_specs=out_specs, check_vma=False
    )
```

```python
import functools
import math

import jax
import jax.numpy as jnp
import numpy as np
from jax import lax
from jax.experimental import pallas as pl
from jax.experimental.pallas import tpu as pltpu
from jax.sharding import PartitionSpec as P


SEG = 2048
FREQ = 512
FLO = 64
LAGS = 256
HALF = 21
CAP = 2
COMP = 3
RADIX = 4
LANE = 128
TILE = 2 * LANE
NONE = -1000
PART = SEG // RADIX
PLANE = 2 * COMP * FREQ
WINDOWS = 2
WIDE = WINDOWS * (PLANE + LANE)
GROUP = 4


def bin_order():
    spot = np.arange(FREQ)
    return RADIX * (spot % LANE) + spot // LANE


def dft_table():
    n1 = np.arange(PART)[:, None]
    blocks = []
    for r in (0, 2, 1, 3):
        k = FLO + RADIX * np.arange(LANE)[None, :] + r
        phase = np.mod(n1 * k, SEG) * (2.0 * math.pi / SEG)
        c, s = np.cos(phase), np.sin(phase)
        blocks.append(np.concatenate([c, -s], 1))
        if r == 1:
            blocks.append(np.concatenate([-s, -c], 1))
        if r == 3:
            blocks.append(np.concatenate([s, c], 1) * np.array([1.0]))
    return np.concatenate(blocks, 0).astype(jnp.bfloat16)


def band_table():
    f = bin_order()
    return (np.abs(f[:, None] - f[None, :]) <= HALF).astype(jnp.bfloat16)


def lag_table():
    bins = FLO + bin_order()[:, None]
    shifts = np.arange(LAGS)[None, :] - LAGS // 2
    phase = np.mod(bins * shifts, SEG) * (2.0 * math.pi / SEG)
    both = np.stack([np.cos(phase), -np.sin(phase)], 0).reshape(2, FREQ // TILE, TILE, LAGS)
    return both.transpose(1, 0, 2, 3).reshape(2 * FREQ, LAGS).astype(jnp.bfloat16)


def mm(a, b):
    return jnp.dot(a, b, preferred_element_type=jnp.float32)


def front_kernel(gaps_hbm, x_hbm, tab_hbm, band_hbm, out_ref, gaps_ref, x_ref, tab_ref, band_ref, sem):
    windows, own = gaps_ref.shape
    rows = windows * own
    parts = tab_ref.shape[0] // PART

    def part_at(i):
        return pl.ds(i * PART, PART)

    loads = [
        pltpu.make_async_copy(x_hbm, x_ref, sem.at[0]),
        *[
            pltpu.make_async_copy(tab_hbm.at[part_at(i)], tab_ref.at[part_at(i)], sem.at[1 + i])
            for i in range(parts)
        ],
        pltpu.make_async_copy(band_hbm, band_ref, sem.at[1 + parts]),
        pltpu.make_async_copy(gaps_hbm, gaps_ref, sem.at[2 + parts]),
    ]
    for load in loads:
        load.start()
    loads[0].wait()
    quarter = []
    for j in range(RADIX):
        per_comp = []
        for a in range(COMP):
            pieces = [
                x_ref[a, :, w * SEG + j * PART : w * SEG + (j + 1) * PART].astype(jnp.float32)
                for w in range(windows)
            ]
            per_comp.append(jnp.concatenate(pieces, 0))
        quarter.append(jnp.concatenate(per_comp, 0))
    x0, x1, x2, x3 = quarter
    even, odd = x0 + x2, x1 + x3

    def halves(y):
        low = y - y.astype(jnp.bfloat16).astype(jnp.float32)
        return jnp.concatenate([y, low], 0).astype(jnp.bfloat16)

    zero, two = halves(even + odd), halves(even - odd)
    u, v = halves(x0 - x2), halves(x1 - x3)

    def tab(i):
        loads[1 + i].wait()
        return tab_ref[part_at(i), :]

    both0 = mm(zero, tab(0))
    both2 = mm(two, tab(1))
    both1 = mm(u, tab(2)) + mm(v, tab(3))
    both3 = mm(u, tab(4)) + mm(v, tab(5))
    both = [both0, both1, both2, both3]
    count = COMP * rows
    spec = [d[:count] + d[count:] for d in both]
    power = []
    for d in spec:
        total = jnp.zeros((rows, LANE), jnp.float32)
        for a in range(COMP):
            re = d[a * rows : (a + 1) * rows, :LANE]
            im = d[a * rows : (a + 1) * rows, LANE:]
            total = total + (re * re + im * im)
        power.append(total)
    power = jnp.concatenate(power, 1)
    p1 = power.astype(jnp.bfloat16).astype(jnp.float32)
    rest = power - p1
    p2 = rest.astype(jnp.bfloat16).astype(jnp.float32)
    p3 = rest - p2
    loads[1 + parts].wait()
    sums = mm(jnp.concatenate([p1, p2, p3], 0).astype(jnp.bfloat16), band_ref[...])
    spot = iota(rows, FREQ, 1)
    f = RADIX * (spot % LANE) + spot // LANE
    taken = jnp.minimum(f + HALF, FREQ - 1) - jnp.maximum(f - HALF, 0) + 1
    share = 1.0 / (taken.astype(jnp.float32) * float(COMP))
    smooth = (sums[:rows] + sums[rows : 2 * rows] + sums[2 * rows :]) * share
    loads[2 + parts].wait()
    row_at = lax.broadcasted_iota(jnp.int32, (rows, LANE), 0)
    flags = jnp.zeros((rows, LANE), jnp.float32)
    for w in range(windows):
        for s in range(own):
            flags = jnp.where(row_at == w * own + s, gaps_ref[w, s].astype(jnp.float32), flags)
    wide_flags = jnp.concatenate([flags] * RADIX, 1)
    factor = wide_flags / jnp.sqrt(smooth + 1e-06)
    for a in range(COMP):
        for part in range(2):
            whole = jnp.concatenate(
                [d[a * rows : (a + 1) * rows, part * LANE : (part + 1) * LANE] for d in spec], 1
            )
            white = whole * factor
            for w in range(windows):
                start = w * PLANE + (2 * a + part) * FREQ
                out_ref[:, start : start + FREQ] = white[w * own : (w + 1) * own].astype(jnp.bfloat16)
    for w in range(windows):
        start = windows * PLANE + w * LANE
        out_ref[:, start : start + LANE] = flags[w * own : (w + 1) * own].astype(jnp.bfloat16)


def front(traces, gaps):
    own, comps, length = traces.shape
    windows = gaps.shape[1]
    assert comps == COMP and length == windows * SEG
    table, band = dft_table(), band_table()
    operands = (gaps.T, traces.transpose(1, 0, 2), jnp.asarray(table), jnp.asarray(band))
    hbm = pl.BlockSpec(memory_space=pltpu.HBM)
    bf16 = jnp.bfloat16
    return pl.pallas_call(
        front_kernel,
        out_shape=jax.ShapeDtypeStruct((own, windows * (PLANE + LANE)), bf16),
        in_specs=[hbm] * 4,
        out_specs=pl.BlockSpec(memory_space=pltpu.VMEM),
        scratch_shapes=[
            pltpu.SMEM((windows, own), jnp.int32),
            pltpu.VMEM((comps, own, length), bf16),
            pltpu.VMEM(table.shape, bf16),
            pltpu.VMEM(band.shape, bf16),
            pltpu.SemaphoreType.DMA((3 + table.shape[0] // PART,)),
        ],
        compiler_params=room(0),
        name="front",
    )(*[pltpu.with_memory_space_constraint(v, pltpu.HBM) for v in operands])


def exchange_plan(count):
    bits = int(count).bit_length() - 1
    assert count == 1 << bits and bits >= 3
    chips = [1 << b for b in range(bits - 1, 0, -1)]
    return [chips, chips[-1:] + chips[:-1]]


def owner_masks(plan):
    own_core = []
    for chips in plan:
        found = [0]
        for m in chips:
            found = found + [f ^ m for f in found]
        own_core.append(found)
    return np.asarray(
        [own_core[p] + [1 ^ f for f in own_core[1 - p]] for p in range(2)], np.int32
    )


def room(operand_bytes):
    return pltpu.CompilerParams(vmem_limit_bytes=(8 << 20) + operand_bytes)


def first_two(flags):
    found = [jnp.int32(NONE)] * CAP
    seen = jnp.int32(0)
    for s, flag in enumerate(flags):
        for c in range(CAP):
            found[c] = jnp.where(jnp.logical_and(flag, seen == c), s, found[c])
        seen = seen + flag.astype(jnp.int32)
    return found


def iota(rows, cols, dim):
    return lax.broadcasted_iota(jnp.int32, (rows, cols), dim)


def one_hot(want, cols):
    return jnp.where(iota(want.shape[0], cols, 1) == want, 1.0, 0.0).astype(jnp.bfloat16)


def own_slots(assign_ref, target_ref, me, own, owner):
    want = target_ref[owner]
    return first_two([assign_ref[me * own + s] == want for s in range(own)])


def spread_kernel(own, assign_ref, target_ref, mask_ref, self_ref, rows_ref, partner_ref):
    me = lax.axis_index("pairs")
    parity = lax.rem(me, 2)
    pairs = GROUP * CAP
    stations = GROUP * own
    mine_rows = self_ref[...]
    rows_ref[...] = mm(one_hot(iota(own * pairs, own, 0) // pairs, own), mine_rows).astype(
        jnp.bfloat16
    )
    place = iota(CAP * stations, own, 0)
    place = (place // stations) * GROUP + (place % stations) // own

    def one_chunk(ch, carry):
        want = jnp.full(place.shape, NONE, jnp.int32)
        for j in range(GROUP):
            owner = me ^ mask_ref[parity, ch * GROUP + j]
            for c, s in enumerate(own_slots(assign_ref, target_ref, me, own, owner)):
                want = jnp.where(place == c * GROUP + j, s, want)
        partner_ref[ch] = mm(one_hot(want, own), mine_rows).astype(jnp.bfloat16)
        return carry

    lax.fori_loop(0, partner_ref.shape[0], one_chunk, 0)


def spread(held, assign, target, masks):
    own = held.shape[0]
    chunks = masks.shape[1] // GROUP
    smem = pl.BlockSpec(memory_space=pltpu.SMEM)
    vmem = pl.BlockSpec(memory_space=pltpu.VMEM)
    made = own * GROUP * CAP + chunks * CAP * GROUP * own
    return pl.pallas_call(
        functools.partial(spread_kernel, own),
        out_shape=(
            jax.ShapeDtypeStruct((own * GROUP * CAP, WIDE), jnp.bfloat16),
            jax.ShapeDtypeStruct((chunks, CAP * GROUP * own, WIDE), jnp.bfloat16),
        ),
        in_specs=[smem] * 3 + [vmem],
        out_specs=(vmem, vmem),
        compiler_params=room(2 * made * WIDE),
        cost_estimate=pl.CostEstimate(
            flops=2 * made * own * WIDE, bytes_accessed=2 * made * WIDE, transcendentals=0
        ),
        name="spread",
    )(assign, target, masks, held)


def correlate_kernel(
    owners, own, windows, base, first, last, assign_ref, target_ref, mask_ref, chunk_ref, rows_ref,
    partner_ref, lag_ref, *rest,
):
    if not first:
        sum_in, rest = rest[0], rest[2:]
    out_ref, sum_ref, picked, cross_e, result_e, cross, result, outv, sem = rest
    me = lax.axis_index("pairs")
    parity = lax.rem(me, 2)
    pairs = GROUP * CAP
    stations = GROUP * own
    nine = COMP * COMP
    chunks = chunk_ref.shape[0] // stations
    my_target = target_ref[me]
    total = jnp.zeros((own, nine * LANE), jnp.float32) if first else sum_in[...]

    def owner_of(ch, j):
        return me ^ mask_ref[parity, base + ch * GROUP + j]

    def copies(ch):
        which = lax.rem(ch, 2)
        return [
            pltpu.make_async_copy(outv.at[which, :, j], out_ref.at[:, owner_of(ch, j)], sem.at[which])
            for j in range(GROUP)
        ]

    def one_chunk(ch, total):
        slot = lax.rem(ch, 2)
        first_row = ch * stations if isinstance(ch, int) else pl.multiple_of(ch * stations, stations)
        here = pl.ds(first_row, stations)
        row = iota(2 * pairs, stations, 0) % pairs
        want = jnp.full(row.shape, NONE, jnp.int32)
        mine = []
        for j in range(GROUP):
            owner = owner_of(ch, j)
            theirs = first_two([assign_ref[owner * own + s] == my_target for s in range(own)])
            for c, s in enumerate(theirs):
                want = jnp.where(row == j * CAP + c, s + j * own, want)
            mine.append(own_slots(assign_ref, target_ref, me, own, owner))
        picked[...] = mm(one_hot(want, stations), chunk_ref[here, :]).astype(jnp.bfloat16)

        def product(left, right):
            re = im = None
            for (lr, li), (rr, ri) in zip(left, right):
                r = lr * rr + li * ri
                i = li * rr - lr * ri
                re = r if re is None else re + r
                im = i if im is None else im + i
            return re, im

        def tile(load, a, lt):
            got = []
            for w in range(windows):
                both = []
                for part in range(2):
                    start = ((w * COMP + a) * 2 + part) * FREQ + lt * TILE
                    both.append(load(slice(start, start + TILE)))
                got.append(both)
            return got

        def partner(rows, lanes):
            return partner_ref[base // GROUP + ch, rows, lanes]

        tiles = FREQ // TILE

        def keep(ref, at, rows, lt, values):
            for part in range(2):
                start = (2 * lt + part) * TILE
                ref[at : at + rows, start : start + TILE] = values[part]

        for lt in range(tiles):
            lefts = [tile(lambda d: chunk_ref[here, d], a, lt) for a in range(COMP)]
            for c in range(CAP):
                part_rows = slice(c * stations, (c + 1) * stations)
                for b in range(COMP):
                    right = tile(lambda d: partner(part_rows, d), b, lt)
                    for a in range(COMP):
                        at = ((c * COMP + a) * COMP + b) * stations
                        keep(cross_e, at, stations, lt, product(lefts[a], right))
        result_e[...] = mm(cross_e[...], lag_ref[...])
        for lt in range(tiles):
            slots = [tile(lambda d: picked[:, d], b, lt) for b in range(COMP)]
            for yp in range(own // 2):
                y_rows = slice(yp * 2 * pairs, (yp + 1) * 2 * pairs)
                for a in range(COMP):
                    left = tile(lambda d: rows_ref[y_rows, d], a, lt)
                    for b in range(COMP):
                        at = ((yp * COMP + a) * COMP + b) * 2 * pairs
                        keep(cross, at, 2 * pairs, lt, product(left, slots[b]))
        result[...] = mm(cross[...], lag_ref[...])

        def flag_at(w):
            return slice(PLANE * windows + w * LANE, PLANE * windows + (w + 1) * LANE)

        weights, squares = [], []
        col = iota(own, stations, 1) // own
        y_row = iota(own, stations, 0)
        for c in range(CAP):
            part_rows = slice(c * stations, (c + 1) * stations)
            weight = jnp.zeros((own, stations), jnp.float32)
            for j in range(GROUP):
                hit = jnp.logical_and(col == j, y_row == mine[j][c])
                weight = jnp.where(hit, 1.0, weight)
            weights.append(weight)
            count = None
            for w in range(windows):
                left = chunk_ref[here, flag_at(w)].astype(jnp.float32)
                term = left * partner(part_rows, flag_at(w)).astype(jnp.float32)
                count = term if count is None else count + term
            most = jnp.maximum(count, 1.0)
            share = 1.0 / (most * most * float(FREQ))
            lines = []
            for q in range(nine):
                at = (c * nine + q) * stations
                block = result_e[at : at + stations, :]
                square = block * block
                both = square[:, :LANE]
                for lt in range(1, LAGS // LANE):
                    both = both + square[:, lt * LANE : (lt + 1) * LANE]
                lines.append(both * share)
            squares.append(jnp.concatenate(lines, 1))
        weights = jnp.concatenate(weights, 1).astype(jnp.bfloat16)
        total = total + mm(weights, jnp.concatenate(squares, 0).astype(jnp.bfloat16))

        if not isinstance(ch, int):

            @pl.when(ch >= 2)
            def _():
                for cp in copies(ch):
                    cp.wait()

        for yp in range(own // 2):
            count = None
            for w in range(windows):
                left = rows_ref[yp * 2 * pairs : (yp + 1) * 2 * pairs, flag_at(w)].astype(jnp.float32)
                term = left * picked[:, flag_at(w)].astype(jnp.float32)
                count = term if count is None else count + term
            scale = 1.0 / (jnp.maximum(count, 1.0) * math.sqrt(FREQ))
            scale = jnp.concatenate([scale] * (LAGS // LANE), 1)
            for q in range(nine):
                at = (yp * nine + q) * 2 * pairs
                block = (result[at : at + 2 * pairs, :] * scale).astype(jnp.bfloat16)
                outv[slot, 2 * yp : 2 * yp + 2, :, q, :, :] = block.reshape(2, GROUP, CAP, LAGS)
        for cp in copies(ch):
            cp.start()
        return total

    if chunks == 1:
        total = one_chunk(0, total)
    else:
        total = lax.fori_loop(0, chunks, one_chunk, total)
    if last:
        lane = iota(own, nine, 1)
        energy = jnp.zeros((own, nine), jnp.float32)
        for q in range(nine):
            part = jnp.sum(total[:, q * LANE : (q + 1) * LANE], axis=1, keepdims=True)
            energy = jnp.where(lane == q, part, energy)
        sum_ref[...] = energy / float(owners * LAGS)
    else:
        sum_ref[...] = total
    for ch in range(max(chunks - 2, 0), chunks):
        for cp in copies(ch):
            cp.wait()


def correlate(chunk, base, spreads, carried, last, assign, target, masks, lags):
    rows, partners = spreads
    owners = target.shape[0]
    own = assign.shape[0] // owners
    windows = (rows.shape[1] - 0) // (PLANE + LANE)
    nine = COMP * COMP
    stations, pairs = GROUP * own, GROUP * CAP
    lines = own * nine * pairs + CAP * nine * stations
    smem = pl.BlockSpec(memory_space=pltpu.SMEM)
    vmem = pl.BlockSpec(memory_space=pltpu.VMEM)
    anywhere = pl.BlockSpec(memory_space=pl.ANY)
    f32, bf16 = jnp.float32, jnp.bfloat16
    first = carried is None
    operands = [assign, target, masks, chunk, rows, partners, lags]
    specs = [smem] * 3 + [vmem] * 4
    aliases = {}
    if not first:
        out_so_far, sums = carried
        operands += [sums, out_so_far]
        specs += [vmem, anywhere]
        aliases = {len(operands) - 1: 0}
    sum_shape = (own, nine) if last else (own, nine * LANE)
    chunks = chunk.shape[0] // stations
    return pl.pallas_call(
        functools.partial(correlate_kernel, owners, own, windows, base, first, last),
        out_shape=(
            jax.ShapeDtypeStruct((own, owners, nine, CAP, LAGS), bf16),
            jax.ShapeDtypeStruct(sum_shape, f32),
        ),
        in_specs=specs,
        out_specs=(anywhere, vmem),
        input_output_aliases=aliases,
        scratch_shapes=[
            pltpu.VMEM((2 * pairs, WIDE), bf16),
            pltpu.VMEM((CAP * nine * stations, 2 * FREQ), bf16),
            pltpu.VMEM((CAP * nine * stations, LAGS), f32),
            pltpu.VMEM((own * nine * pairs, 2 * FREQ), bf16),
            pltpu.VMEM((own * nine * pairs, LAGS), f32),
            pltpu.VMEM((2, own, GROUP, nine, CAP, LAGS), bf16),
            pltpu.SemaphoreType.DMA((2,)),
        ],
        compiler_params=room(2 * (chunk.size + rows.size + partners.size)),
        cost_estimate=pl.CostEstimate(
            flops=chunks * 4 * lines * FREQ * LAGS,
            bytes_accessed=chunks * 2 * lines * LAGS,
            transcendentals=0,
        ),
        name="correlate",
    )(*operands)


def steps_of(traces, gaps, assign, target):
    owners = lax.axis_size("pairs")
    plan = exchange_plan(owners)
    masks = jnp.asarray(owner_masks(plan))
    lags = jnp.asarray(lag_table())

    def swap(block, masks_of):
        return lax.ppermute(block, "pairs", [(i, i ^ masks_of[i % 2]) for i in range(owners)])

    steps = [tuple(m) for m in zip(*plan)]
    held = front(traces, gaps)
    spreads = spread(held, assign, target, masks)
    for step in steps[:2]:
        got = swap(held, step)
        held = jnp.concatenate([held, got], 0)
    blocks = [held]
    for step in steps[2:]:
        sent = jnp.concatenate(blocks, 0) if len(blocks) > 1 else held
        blocks.append(swap(sent, step))
    other = []
    for block in blocks:
        other.append(swap(block, (1, 1)))
    base = 0
    order = []
    for block in blocks + other:
        order.append((block, base))
        base += block.shape[0] // traces.shape[0]
    count = len(blocks)
    ranked = [order[i + side * count] for i in range(count) for side in range(2)]
    carried = None
    for at, (block, start) in enumerate(ranked):
        last = at == len(ranked) - 1
        carried = correlate(block, start, spreads, carried, last, assign, target, masks, lags)
    out, energy = carried
    return out.transpose(0, 1, 3, 2, 4), energy


def solution(mesh):
    in_specs = (
        P(("groups", "pairs"), None, None),
        P(("groups", "pairs"), None),
        P("groups"),
        P("groups"),
    )
    out_specs = (P(("groups", "pairs"), None, None, None, None), P(("groups", "pairs"), None))
    return jax.shard_map(
        steps_of, mesh=mesh, in_specs=in_specs, out_specs=out_specs, check_vma=False
    )
```

```python
import functools
import math

import jax
import jax.numpy as jnp
import numpy as np
from jax import lax
from jax.experimental import pallas as pl
from jax.experimental.pallas import tpu as pltpu
from jax.sharding import PartitionSpec as P


SEG = 2048
FREQ = 512
FLO = 64
LAGS = 256
HALF = 21
CAP = 2
COMP = 3
RADIX = 4
LANE = 128
TILE = 2 * LANE
NONE = -1000
PART = SEG // RADIX
PLANE = 2 * COMP * FREQ
WINDOWS = 2
WIDE = WINDOWS * (PLANE + LANE)
GROUP = 4


def bin_order():
    spot = np.arange(FREQ)
    return RADIX * (spot % LANE) + spot // LANE


def dft_table():
    n1 = np.arange(PART)[:, None]
    blocks = []
    for r in (0, 2, 1, 3):
        k = FLO + RADIX * np.arange(LANE)[None, :] + r
        phase = np.mod(n1 * k, SEG) * (2.0 * math.pi / SEG)
        c, s = np.cos(phase), np.sin(phase)
        blocks.append(np.concatenate([c, -s], 1))
        if r == 1:
            blocks.append(np.concatenate([-s, -c], 1))
        if r == 3:
            blocks.append(np.concatenate([s, c], 1) * np.array([1.0]))
    return np.concatenate(blocks, 0).astype(jnp.bfloat16)


def band_table():
    f = bin_order()
    return (np.abs(f[:, None] - f[None, :]) <= HALF).astype(jnp.bfloat16)


def lag_table():
    bins = FLO + bin_order()[:, None]
    shifts = np.arange(LAGS)[None, :] - LAGS // 2
    phase = np.mod(bins * shifts, SEG) * (2.0 * math.pi / SEG)
    both = np.stack([np.cos(phase), -np.sin(phase)], 0).reshape(2, FREQ // TILE, TILE, LAGS)
    return both.transpose(1, 0, 2, 3).reshape(2 * FREQ, LAGS).astype(jnp.bfloat16)


def mm(a, b):
    return jnp.dot(a, b, preferred_element_type=jnp.float32)


def front_kernel(gaps_hbm, x_hbm, tab_hbm, band_hbm, out_ref, gaps_ref, x_ref, tab_ref, band_ref, sem):
    windows, own = gaps_ref.shape
    rows = windows * own
    parts = tab_ref.shape[0] // PART

    def part_at(i):
        return pl.ds(i * PART, PART)

    loads = [
        pltpu.make_async_copy(x_hbm, x_ref, sem.at[0]),
        *[
            pltpu.make_async_copy(tab_hbm.at[part_at(i)], tab_ref.at[part_at(i)], sem.at[1 + i])
            for i in range(parts)
        ],
        pltpu.make_async_copy(band_hbm, band_ref, sem.at[1 + parts]),
        pltpu.make_async_copy(gaps_hbm, gaps_ref, sem.at[2 + parts]),
    ]
    for load in loads:
        load.start()
    loads[0].wait()
    quarter = []
    for j in range(RADIX):
        per_comp = []
        for a in range(COMP):
            pieces = [
                x_ref[a, :, w * SEG + j * PART : w * SEG + (j + 1) * PART].astype(jnp.float32)
                for w in range(windows)
            ]
            per_comp.append(jnp.concatenate(pieces, 0))
        quarter.append(jnp.concatenate(per_comp, 0))
    x0, x1, x2, x3 = quarter
    even, odd = x0 + x2, x1 + x3

    def halves(y):
        low = y - y.astype(jnp.bfloat16).astype(jnp.float32)
        return jnp.concatenate([y, low], 0).astype(jnp.bfloat16)

    zero, two = halves(even + odd), halves(even - odd)
    u, v = halves(x0 - x2), halves(x1 - x3)

    def tab(i):
        loads[1 + i].wait()
        return tab_ref[part_at(i), :]

    both0 = mm(zero, tab(0))
    both2 = mm(two, tab(1))
    both1 = mm(u, tab(2)) + mm(v, tab(3))
    both3 = mm(u, tab(4)) + mm(v, tab(5))
    both = [both0, both1, both2, both3]
    count = COMP * rows
    spec = [d[:count] + d[count:] for d in both]
    power = []
    for d in spec:
        total = jnp.zeros((rows, LANE), jnp.float32)
        for a in range(COMP):
            re = d[a * rows : (a + 1) * rows, :LANE]
            im = d[a * rows : (a + 1) * rows, LANE:]
            total = total + (re * re + im * im)
        power.append(total)
    power = jnp.concatenate(power, 1)
    p1 = power.astype(jnp.bfloat16).astype(jnp.float32)
    rest = power - p1
    p2 = rest.astype(jnp.bfloat16).astype(jnp.float32)
    p3 = rest - p2
    loads[1 + parts].wait()
    sums = mm(jnp.concatenate([p1, p2, p3], 0).astype(jnp.bfloat16), band_ref[...])
    spot = iota(rows, FREQ, 1)
    f = RADIX * (spot % LANE) + spot // LANE
    taken = jnp.minimum(f + HALF, FREQ - 1) - jnp.maximum(f - HALF, 0) + 1
    share = 1.0 / (taken.astype(jnp.float32) * float(COMP))
    smooth = (sums[:rows] + sums[rows : 2 * rows] + sums[2 * rows :]) * share
    loads[2 + parts].wait()
    row_at = lax.broadcasted_iota(jnp.int32, (rows, LANE), 0)
    flags = jnp.zeros((rows, LANE), jnp.float32)
    for w in range(windows):
        for s in range(own):
            flags = jnp.where(row_at == w * own + s, gaps_ref[w, s].astype(jnp.float32), flags)
    wide_flags = jnp.concatenate([flags] * RADIX, 1)
    factor = wide_flags / jnp.sqrt(smooth + 1e-06)
    for a in range(COMP):
        for part in range(2):
            whole = jnp.concatenate(
                [d[a * rows : (a + 1) * rows, part * LANE : (part + 1) * LANE] for d in spec], 1
            )
            white = whole * factor
            for w in range(windows):
                start = w * PLANE + (2 * a + part) * FREQ
                out_ref[:, start : start + FREQ] = white[w * own : (w + 1) * own].astype(jnp.bfloat16)
    for w in range(windows):
        start = windows * PLANE + w * LANE
        out_ref[:, start : start + LANE] = flags[w * own : (w + 1) * own].astype(jnp.bfloat16)


def front(traces, gaps):
    own, comps, length = traces.shape
    windows = gaps.shape[1]
    assert comps == COMP and length == windows * SEG
    table, band = dft_table(), band_table()
    operands = (gaps.T, traces.transpose(1, 0, 2), jnp.asarray(table), jnp.asarray(band))
    hbm = pl.BlockSpec(memory_space=pltpu.HBM)
    bf16 = jnp.bfloat16
    return pl.pallas_call(
        front_kernel,
        out_shape=jax.ShapeDtypeStruct((own, windows * (PLANE + LANE)), bf16),
        in_specs=[hbm] * 4,
        out_specs=pl.BlockSpec(memory_space=pltpu.VMEM),
        scratch_shapes=[
            pltpu.SMEM((windows, own), jnp.int32),
            pltpu.VMEM((comps, own, length), bf16),
            pltpu.VMEM(table.shape, bf16),
            pltpu.VMEM(band.shape, bf16),
            pltpu.SemaphoreType.DMA((3 + table.shape[0] // PART,)),
        ],
        compiler_params=room(0),
        name="front",
    )(*[pltpu.with_memory_space_constraint(v, pltpu.HBM) for v in operands])


def exchange_plan(count):
    bits = int(count).bit_length() - 1
    assert count == 1 << bits and bits >= 3
    chips = [1 << b for b in range(bits - 1, 0, -1)]
    return [chips, chips[-1:] + chips[:-1]]


def owner_at(plan, me, place):
    parity = lax.rem(me, 2)
    bits = len(plan[0])
    if isinstance(place, int):
        found = []
        for p in range(2):
            far = place >> bits
            mask = far
            for i, m in enumerate(plan[p ^ far]):
                mask ^= m * ((place >> i) & 1)
            found.append(mask)
        return me ^ jnp.where(parity == 0, found[0], found[1])
    far = place >> bits
    side = parity ^ far
    mask = far
    for i in range(bits):
        step = jnp.where(side == 0, plan[0][i], plan[1][i])
        mask = mask ^ (step * ((place >> i) & 1))
    return me ^ mask


def room(operand_bytes):
    return pltpu.CompilerParams(vmem_limit_bytes=(8 << 20) + operand_bytes)


def first_two(flags):
    found = [jnp.int32(NONE)] * CAP
    seen = jnp.int32(0)
    for s, flag in enumerate(flags):
        for c in range(CAP):
            found[c] = jnp.where(jnp.logical_and(flag, seen == c), s, found[c])
        seen = seen + flag.astype(jnp.int32)
    return found


def iota(rows, cols, dim):
    return lax.broadcasted_iota(jnp.int32, (rows, cols), dim)


def one_hot(want, cols):
    return jnp.where(iota(want.shape[0], cols, 1) == want, 1.0, 0.0).astype(jnp.bfloat16)


def spread_kernel(plan, own, assign_ref, target_ref, self_ref, rows_ref, partner_ref, pick_ref, weight_ref):
    me = lax.axis_index("pairs")
    pairs = GROUP * CAP
    stations = GROUP * own
    mine_rows = self_ref[...]
    rows_ref[...] = mm(one_hot(iota(own * pairs, own, 0) // pairs, own), mine_rows).astype(
        jnp.bfloat16
    )
    place = iota(CAP * stations, own, 0)
    place = (place // stations) * GROUP + (place % stations) // own
    slot = iota(2 * pairs, stations, 0) % pairs
    col = iota(own, CAP * stations, 1)
    col = (col // stations) * GROUP + (col % stations) // own
    y_row = iota(own, CAP * stations, 0)
    my_target = target_ref[me]

    def one_chunk(ch, carry):
        want = jnp.full(place.shape, NONE, jnp.int32)
        taken = jnp.full(slot.shape, NONE, jnp.int32)
        weight = jnp.zeros(col.shape, jnp.float32)
        for j in range(GROUP):
            owner = owner_at(plan, me, ch * GROUP + j)
            wanted = target_ref[owner]
            mine = first_two([assign_ref[me * own + s] == wanted for s in range(own)])
            theirs = first_two([assign_ref[owner * own + s] == my_target for s in range(own)])
            for c in range(CAP):
                want = jnp.where(place == c * GROUP + j, mine[c], want)
                hit = jnp.logical_and(col == c * GROUP + j, y_row == mine[c])
                weight = jnp.where(hit, 1.0, weight)
                taken = jnp.where(slot == j * CAP + c, theirs[c] + j * own, taken)
        partner_ref[ch] = mm(one_hot(want, own), mine_rows).astype(jnp.bfloat16)
        pick_ref[ch] = one_hot(taken, stations)
        weight_ref[ch] = weight.astype(jnp.bfloat16)
        return carry

    lax.fori_loop(0, partner_ref.shape[0], one_chunk, 0)


def spread(plan, held, assign, target):
    own = held.shape[0]
    chunks = target.shape[0] // GROUP
    stations, pairs = GROUP * own, GROUP * CAP
    smem = pl.BlockSpec(memory_space=pltpu.SMEM)
    vmem = pl.BlockSpec(memory_space=pltpu.VMEM)
    made = own * pairs + chunks * CAP * stations
    bf16 = jnp.bfloat16
    return pl.pallas_call(
        functools.partial(spread_kernel, plan, own),
        out_shape=(
            jax.ShapeDtypeStruct((own * pairs, WIDE), bf16),
            jax.ShapeDtypeStruct((chunks, CAP * stations, WIDE), bf16),
            jax.ShapeDtypeStruct((chunks, 2 * pairs, stations), bf16),
            jax.ShapeDtypeStruct((chunks, own, CAP * stations), bf16),
        ),
        in_specs=[smem] * 2 + [vmem],
        out_specs=(vmem,) * 4,
        compiler_params=room(2 * made * WIDE),
        cost_estimate=pl.CostEstimate(
            flops=2 * made * own * WIDE, bytes_accessed=2 * made * WIDE, transcendentals=0
        ),
        name="spread",
    )(assign, target, held)


def correlate_kernel(plan, owners, own, windows, base, kind, chunk_ref, *refs):
    refs = list(refs)
    rows_ref, partner_ref, pick_ref, weight_ref, lag_ref = refs[:5]
    refs = refs[5:]
    sum_in = refs.pop(0) if kind["sums"] else None
    waiting = refs.pop(0) if kind["waiting"] is not None else None
    if kind["out_in"]:
        refs.pop(0)
    out_ref = refs.pop(0) if kind["out"] else None
    kept = refs.pop(0) if kind["keep"] else None
    sum_ref = refs.pop(0)
    picked, cross_e, result_e, cross, result, outv, energy_v, sem = refs
    me = lax.axis_index("pairs")
    pairs = GROUP * CAP
    stations = GROUP * own
    nine = COMP * COMP
    chunks = chunk_ref.shape[0] // stations
    total = sum_in[...] if kind["sums"] else jnp.zeros((own, nine * LANE), jnp.float32)

    def flush(source, place, which, ys=slice(None)):
        return [
            pltpu.make_async_copy(
                source.at[ys, j], out_ref.at[ys, owner_at(plan, me, place + j)], sem.at[which]
            )
            for j in range(GROUP)
        ]

    def copies(ch):
        return flush(outv.at[lax.rem(ch, 2)], base + ch * GROUP, lax.rem(ch, 2))

    before = [] if waiting is None else flush(waiting, kind["waiting"], 2)
    for cp in before:
        cp.start()
    started = []

    def one_chunk(ch, total):
        slot = lax.rem(ch, 2)
        first_row = ch * stations if isinstance(ch, int) else pl.multiple_of(ch * stations, stations)
        here = pl.ds(first_row, stations)
        number = base // GROUP + ch
        picked[...] = mm(pick_ref[number], chunk_ref[here, :]).astype(jnp.bfloat16)

        def product(left, right):
            re = im = None
            for (lr, li), (rr, ri) in zip(left, right):
                r = lr * rr + li * ri
                i = li * rr - lr * ri
                re = r if re is None else re + r
                im = i if im is None else im + i
            return re, im

        def tile(load, a, lt):
            got = []
            for w in range(windows):
                both = []
                for part in range(2):
                    start = ((w * COMP + a) * 2 + part) * FREQ + lt * TILE
                    both.append(load(slice(start, start + TILE)))
                got.append(both)
            return got

        def partner(rows, lanes):
            return partner_ref[number, rows, lanes]

        tiles = FREQ // TILE

        def keep(ref, at, rows, lt, values):
            for part in range(2):
                start = (2 * lt + part) * TILE
                ref[at : at + rows, start : start + TILE] = values[part]

        for lt in range(tiles):
            lefts = [tile(lambda d: chunk_ref[here, d], a, lt) for a in range(COMP)]
            for c in range(CAP):
                part_rows = slice(c * stations, (c + 1) * stations)
                for b in range(COMP):
                    right = tile(lambda d: partner(part_rows, d), b, lt)
                    for a in range(COMP):
                        at = ((c * COMP + a) * COMP + b) * stations
                        keep(cross_e, at, stations, lt, product(lefts[a], right))
        result_e[...] = mm(cross_e[...], lag_ref[...])
        for lt in range(tiles):
            slots = [tile(lambda d: picked[:, d], b, lt) for b in range(COMP)]
            for yp in range(own // 2):
                y_rows = slice(yp * 2 * pairs, (yp + 1) * 2 * pairs)
                for a in range(COMP):
                    left = tile(lambda d: rows_ref[y_rows, d], a, lt)
                    for b in range(COMP):
                        at = ((yp * COMP + a) * COMP + b) * 2 * pairs
                        keep(cross, at, 2 * pairs, lt, product(left, slots[b]))
        result[...] = mm(cross[...], lag_ref[...])

        def flag_at(w):
            return slice(PLANE * windows + w * LANE, PLANE * windows + (w + 1) * LANE)

        squares = []
        for c in range(CAP):
            part_rows = slice(c * stations, (c + 1) * stations)
            count = None
            for w in range(windows):
                left = chunk_ref[here, flag_at(w)].astype(jnp.float32)
                term = left * partner(part_rows, flag_at(w)).astype(jnp.float32)
                count = term if count is None else count + term
            most = jnp.maximum(count, 1.0)
            share = 1.0 / (most * most * float(FREQ))
            lines = []
            for q in range(nine):
                at = (c * nine + q) * stations
                block = result_e[at : at + stations, :]
                square = block * block
                both = square[:, :LANE]
                for lt in range(1, LAGS // LANE):
                    both = both + square[:, lt * LANE : (lt + 1) * LANE]
                lines.append(both * share)
            squares.append(jnp.concatenate(lines, 1))
        total = total + mm(weight_ref[number], jnp.concatenate(squares, 0).astype(jnp.bfloat16))
        if kind["last"] and chunks == 1:
            finish(total)

        if not isinstance(ch, int):

            @pl.when(ch >= 2)
            def _():
                for cp in copies(ch):
                    cp.wait()

        for yp in range(own // 2):
            count = None
            for w in range(windows):
                left = rows_ref[yp * 2 * pairs : (yp + 1) * 2 * pairs, flag_at(w)].astype(jnp.float32)
                term = left * picked[:, flag_at(w)].astype(jnp.float32)
                count = term if count is None else count + term
            scale = 1.0 / (jnp.maximum(count, 1.0) * math.sqrt(FREQ))
            scale = jnp.concatenate([scale] * (LAGS // LANE), 1)
            ys = slice(2 * yp, 2 * yp + 2)
            for q in range(nine):
                at = (yp * nine + q) * 2 * pairs
                block = (result[at : at + 2 * pairs, :] * scale).astype(jnp.bfloat16)
                block = block.reshape(2, GROUP, CAP, LAGS)
                if kind["keep"]:
                    kept[ys, :, q, :, :] = block
                else:
                    outv[slot, ys, :, q, :, :] = block
            if chunks == 1 and not kind["keep"]:
                for cp in flush(outv.at[0], base, 0, ys):
                    cp.start()
                    started.append(cp)
        if chunks > 1:
            for cp in copies(ch):
                cp.start()
        return total

    def finish(total):
        lane = iota(own, nine, 1)
        energy = jnp.zeros((own, nine), jnp.float32)
        for q in range(nine):
            part = jnp.sum(total[:, q * LANE : (q + 1) * LANE], axis=1, keepdims=True)
            energy = jnp.where(lane == q, part, energy)
        energy_v[...] = energy / float(owners * LAGS)
        cp = pltpu.make_async_copy(energy_v, sum_ref, sem.at[3])
        cp.start()
        started.append(cp)

    if chunks == 1:
        total = one_chunk(0, total)
    else:
        total = lax.fori_loop(0, chunks, one_chunk, total)
        if kind["last"]:
            finish(total)
    if not kind["last"]:
        sum_ref[...] = total
    for cp in before + started:
        cp.wait()
    if chunks > 1:
        for ch in range(chunks - 2, chunks):
            for cp in copies(ch):
                cp.wait()


def correlate(plan, block, base, spreads, lags, carried, last, owners, windows):
    own = spreads[3].shape[1]
    nine = COMP * COMP
    stations, pairs = GROUP * own, GROUP * CAP
    vmem = pl.BlockSpec(memory_space=pltpu.VMEM)
    anywhere = pl.BlockSpec(memory_space=pl.ANY)
    f32, bf16 = jnp.float32, jnp.bfloat16
    chunks = block.shape[0] // stations
    sums, waiting, waiting_base, out_so_far = carried
    kind = {
        "last": last,
        "sums": sums is not None,
        "waiting": waiting_base,
        "out_in": out_so_far is not None,
        "keep": chunks == 1 and not last,
    }
    kind["out"] = waiting is not None or out_so_far is not None or not kind["keep"]
    operands, specs, aliases = [block, *spreads, lags], [vmem] * 6, {}
    if kind["sums"]:
        operands.append(sums)
        specs.append(vmem)
    if waiting is not None:
        operands.append(waiting)
        specs.append(vmem)
    if kind["out_in"]:
        aliases = {len(operands): 0}
        operands.append(out_so_far)
        specs.append(anywhere)
    shapes, out_specs = [], []
    if kind["out"]:
        shapes.append(jax.ShapeDtypeStruct((own, owners, nine, CAP, LAGS), bf16))
        out_specs.append(anywhere)
    if kind["keep"]:
        shapes.append(jax.ShapeDtypeStruct((own, GROUP, nine, CAP, LAGS), bf16))
        out_specs.append(vmem)
    shapes.append(jax.ShapeDtypeStruct((own, nine) if last else (own, nine * LANE), f32))
    out_specs.append(anywhere if last else vmem)
    half = CAP * nine * stations
    results = pl.pallas_call(
        functools.partial(correlate_kernel, plan, owners, own, windows, base, kind),
        out_shape=tuple(shapes),
        in_specs=specs,
        out_specs=tuple(out_specs),
        input_output_aliases=aliases,
        scratch_shapes=[
            pltpu.VMEM((2 * pairs, WIDE), bf16),
            pltpu.VMEM((half, 2 * FREQ), bf16),
            pltpu.VMEM((half, LAGS), f32),
            pltpu.VMEM((own * nine * pairs, 2 * FREQ), bf16),
            pltpu.VMEM((own * nine * pairs, LAGS), f32),
            pltpu.VMEM((2, own, GROUP, nine, CAP, LAGS), bf16),
            pltpu.VMEM((own, nine), f32),
            pltpu.SemaphoreType.DMA((4,)),
        ],
        compiler_params=room(2 * (block.size + sum(v.size for v in spreads))),
        cost_estimate=pl.CostEstimate(
            flops=chunks * 8 * half * FREQ * LAGS,
            bytes_accessed=chunks * 4 * half * LAGS,
            transcendentals=0,
        ),
        name="correlate",
    )(*operands)
    results = list(results)
    out = results.pop(0) if kind["out"] else None
    kept = results.pop(0) if kind["keep"] else None
    return results[0], kept, base if kind["keep"] else None, out


def steps_of(traces, gaps, assign, target):
    owners = lax.axis_size("pairs")
    own, windows = gaps.shape
    plan = exchange_plan(owners)
    lags = jnp.asarray(lag_table())

    def swap(block, masks_of):
        return lax.ppermute(block, "pairs", [(i, i ^ masks_of[i % 2]) for i in range(owners)])

    steps = [tuple(m) for m in zip(*plan)]
    held = front(traces, gaps)
    spreads = spread(plan, held, assign, target)
    for step in steps[:2]:
        got = swap(held, step)
        held = jnp.concatenate([held, got], 0)
    blocks = [held]
    for step in steps[2:]:
        sent = jnp.concatenate(blocks, 0) if len(blocks) > 1 else held
        blocks.append(swap(sent, step))
    other = []
    for block in blocks:
        other.append(swap(block, (1, 1)))
    base = 0
    order = []
    for block in blocks + other:
        order.append((block, base))
        base += block.shape[0] // own
    count = len(blocks)
    ranked = [order[i + side * count] for i in range(count) for side in range(2)]
    carried = (None, None, None, None)
    for at, (block, start) in enumerate(ranked):
        last = at == len(ranked) - 1
        carried = correlate(plan, block, start, spreads, lags, carried, last, owners, windows)
    energy, _, _, out = carried
    return out.transpose(0, 1, 3, 2, 4), energy


def solution(mesh):
    in_specs = (
        P(("groups", "pairs"), None, None),
        P(("groups", "pairs"), None),
        P("groups"),
        P("groups"),
    )
    out_specs = (P(("groups", "pairs"), None, None, None, None), P(("groups", "pairs"), None))
    return jax.shard_map(
        steps_of, mesh=mesh, in_specs=in_specs, out_specs=out_specs, check_vma=False
    )
```

```python
import functools
import math

import jax
import jax.numpy as jnp
import numpy as np
from jax import lax
from jax.experimental import pallas as pl
from jax.experimental.pallas import tpu as pltpu
from jax.sharding import PartitionSpec as P


SEG = 2048
FREQ = 512
FLO = 64
LAGS = 256
HALF = 21
CAP = 2
COMP = 3
RADIX = 4
LANE = 128
TILE = 2 * LANE
NONE = -1000
PART = SEG // RADIX
PLANE = 2 * COMP * FREQ
WINDOWS = 2
WIDE = WINDOWS * (PLANE + LANE)
GROUP = 4


def bin_order():
    spot = np.arange(FREQ)
    return RADIX * (spot % LANE) + spot // LANE


def dft_table():
    n1 = np.arange(PART)[:, None]
    blocks = []
    for r in (0, 2, 1, 3):
        k = FLO + RADIX * np.arange(LANE)[None, :] + r
        phase = np.mod(n1 * k, SEG) * (2.0 * math.pi / SEG)
        c, s = np.cos(phase), np.sin(phase)
        blocks.append(np.concatenate([c, -s], 1))
        if r == 1:
            blocks.append(np.concatenate([-s, -c], 1))
        if r == 3:
            blocks.append(np.concatenate([s, c], 1) * np.array([1.0]))
    return np.concatenate(blocks, 0).astype(jnp.bfloat16)


def band_table():
    f = bin_order()
    return (np.abs(f[:, None] - f[None, :]) <= HALF).astype(jnp.bfloat16)


def lag_table():
    bins = FLO + bin_order()[:, None]
    shifts = np.arange(LAGS)[None, :] - LAGS // 2
    phase = np.mod(bins * shifts, SEG) * (2.0 * math.pi / SEG)
    both = np.stack([np.cos(phase), -np.sin(phase)], 0).reshape(2, FREQ // TILE, TILE, LAGS)
    return both.transpose(1, 0, 2, 3).reshape(2 * FREQ, LAGS).astype(jnp.bfloat16)


def mm(a, b):
    return jnp.dot(a, b, preferred_element_type=jnp.float32)


def exchange_plan(count):
    bits = int(count).bit_length() - 1
    assert count == 1 << bits and bits >= 4
    chips = [1 << b for b in range(bits - 1, 0, -1)]
    return chips[:1] + chips[-1:] + chips[1:-1]


def owner_at(plan, me, place):
    mask = place >> len(plan)
    for i, m in enumerate(plan):
        mask = mask ^ (m * ((place >> i) & 1))
    return me ^ mask


def room(operand_bytes):
    return pltpu.CompilerParams(vmem_limit_bytes=(8 << 20) + operand_bytes)


def first_two(flags):
    found = [jnp.int32(NONE)] * CAP
    seen = jnp.int32(0)
    for s, flag in enumerate(flags):
        for c in range(CAP):
            found[c] = jnp.where(jnp.logical_and(flag, seen == c), s, found[c])
        seen = seen + flag.astype(jnp.int32)
    return found


def iota(rows, cols, dim):
    return lax.broadcasted_iota(jnp.int32, (rows, cols), dim)


def one_hot(want, cols):
    return jnp.where(iota(want.shape[0], cols, 1) == want, 1.0, 0.0).astype(jnp.bfloat16)


def meet(plan, own, assign_ref, target_ref, pick_ref, mine_ref, weight_ref):
    me = lax.axis_index("pairs")
    pairs = GROUP * CAP
    stations = GROUP * own
    place = iota(CAP * stations, own, 0)
    place = (place // stations) * GROUP + (place % stations) // own
    slot = iota(2 * pairs, stations, 0) % pairs
    col = iota(own, CAP * stations, 1)
    col = (col // stations) * GROUP + (col % stations) // own
    y_row = iota(own, CAP * stations, 0)
    my_target = target_ref[me]

    def one_group(ch, carry):
        want = jnp.full(place.shape, NONE, jnp.int32)
        taken = jnp.full(slot.shape, NONE, jnp.int32)
        weight = jnp.zeros(col.shape, jnp.float32)
        for j in range(GROUP):
            owner = owner_at(plan, me, ch * GROUP + j)
            wanted = target_ref[owner]
            mine = first_two([assign_ref[me * own + s] == wanted for s in range(own)])
            theirs = first_two([assign_ref[owner * own + s] == my_target for s in range(own)])
            for c in range(CAP):
                want = jnp.where(place == c * GROUP + j, mine[c], want)
                hit = jnp.logical_and(col == c * GROUP + j, y_row == mine[c])
                weight = jnp.where(hit, 1.0, weight)
                taken = jnp.where(slot == j * CAP + c, theirs[c] + j * own, taken)
        mine_ref[ch] = one_hot(want, own)
        pick_ref[ch] = one_hot(taken, stations)
        weight_ref[ch] = weight.astype(jnp.bfloat16)
        return carry

    lax.fori_loop(0, pick_ref.shape[0], one_group, 0)


def front_kernel(
    plan, gaps_hbm, assign_hbm, target_hbm, x_hbm, tab_hbm, band_hbm, out_ref, pick_ref, mine_ref,
    weight_ref, gaps_ref, assign_ref, target_ref, x_ref, tab_ref, band_ref, sem,
):
    windows, own = gaps_ref.shape
    rows = windows * own
    parts = tab_ref.shape[0] // PART

    def part_at(i):
        return pl.ds(i * PART, PART)

    loads = [
        pltpu.make_async_copy(x_hbm, x_ref, sem.at[0]),
        *[
            pltpu.make_async_copy(tab_hbm.at[part_at(i)], tab_ref.at[part_at(i)], sem.at[1 + i])
            for i in range(parts)
        ],
        pltpu.make_async_copy(band_hbm, band_ref, sem.at[1 + parts]),
        pltpu.make_async_copy(gaps_hbm, gaps_ref, sem.at[2 + parts]),
    ]
    names = [
        pltpu.make_async_copy(assign_hbm, assign_ref, sem.at[3 + parts]),
        pltpu.make_async_copy(target_hbm, target_ref, sem.at[4 + parts]),
    ]
    for load in names + loads:
        load.start()
    for load in names:
        load.wait()
    meet(plan, own, assign_ref, target_ref, pick_ref, mine_ref, weight_ref)
    loads[0].wait()
    quarter = []
    for j in range(RADIX):
        per_comp = []
        for a in range(COMP):
            pieces = [
                x_ref[a, :, w * SEG + j * PART : w * SEG + (j + 1) * PART].astype(jnp.float32)
                for w in range(windows)
            ]
            per_comp.append(jnp.concatenate(pieces, 0))
        quarter.append(jnp.concatenate(per_comp, 0))
    x0, x1, x2, x3 = quarter
    even, odd = x0 + x2, x1 + x3

    def halves(y):
        low = y - y.astype(jnp.bfloat16).astype(jnp.float32)
        return jnp.concatenate([y, low], 0).astype(jnp.bfloat16)

    zero, two = halves(even + odd), halves(even - odd)
    u, v = halves(x0 - x2), halves(x1 - x3)

    def tab(i):
        loads[1 + i].wait()
        return tab_ref[part_at(i), :]

    both0 = mm(zero, tab(0))
    both2 = mm(two, tab(1))
    both1 = mm(u, tab(2)) + mm(v, tab(3))
    both3 = mm(u, tab(4)) + mm(v, tab(5))
    both = [both0, both1, both2, both3]
    count = COMP * rows
    spec = [d[:count] + d[count:] for d in both]
    power = []
    for d in spec:
        total = jnp.zeros((rows, LANE), jnp.float32)
        for a in range(COMP):
            re = d[a * rows : (a + 1) * rows, :LANE]
            im = d[a * rows : (a + 1) * rows, LANE:]
            total = total + (re * re + im * im)
        power.append(total)
    power = jnp.concatenate(power, 1)
    p1 = power.astype(jnp.bfloat16).astype(jnp.float32)
    rest = power - p1
    p2 = rest.astype(jnp.bfloat16).astype(jnp.float32)
    p3 = rest - p2
    loads[1 + parts].wait()
    sums = mm(jnp.concatenate([p1, p2, p3], 0).astype(jnp.bfloat16), band_ref[...])
    spot = iota(rows, FREQ, 1)
    f = RADIX * (spot % LANE) + spot // LANE
    taken = jnp.minimum(f + HALF, FREQ - 1) - jnp.maximum(f - HALF, 0) + 1
    share = 1.0 / (taken.astype(jnp.float32) * float(COMP))
    smooth = (sums[:rows] + sums[rows : 2 * rows] + sums[2 * rows :]) * share
    loads[2 + parts].wait()
    row_at = lax.broadcasted_iota(jnp.int32, (rows, LANE), 0)
    flags = jnp.zeros((rows, LANE), jnp.float32)
    for w in range(windows):
        for s in range(own):
            flags = jnp.where(row_at == w * own + s, gaps_ref[w, s].astype(jnp.float32), flags)
    wide_flags = jnp.concatenate([flags] * RADIX, 1)
    factor = wide_flags / jnp.sqrt(smooth + 1e-06)
    for a in range(COMP):
        for part in range(2):
            whole = jnp.concatenate(
                [d[a * rows : (a + 1) * rows, part * LANE : (part + 1) * LANE] for d in spec], 1
            )
            white = whole * factor
            for w in range(windows):
                start = w * PLANE + (2 * a + part) * FREQ
                out_ref[:, start : start + FREQ] = white[w * own : (w + 1) * own].astype(jnp.bfloat16)
    for w in range(windows):
        start = windows * PLANE + w * LANE
        out_ref[:, start : start + LANE] = flags[w * own : (w + 1) * own].astype(jnp.bfloat16)


def front(plan, traces, gaps, assign, target):
    own, comps, length = traces.shape
    windows = gaps.shape[1]
    assert comps == COMP and length == windows * SEG
    table, band = dft_table(), band_table()
    operands = (gaps.T, assign, target, traces.transpose(1, 0, 2), jnp.asarray(table), jnp.asarray(band))
    hbm = pl.BlockSpec(memory_space=pltpu.HBM)
    vmem = pl.BlockSpec(memory_space=pltpu.VMEM)
    bf16 = jnp.bfloat16
    groups, stations = target.shape[0] // GROUP, GROUP * own
    return pl.pallas_call(
        functools.partial(front_kernel, plan),
        out_shape=(
            jax.ShapeDtypeStruct((own, windows * (PLANE + LANE)), bf16),
            jax.ShapeDtypeStruct((groups, 2 * GROUP * CAP, stations), bf16),
            jax.ShapeDtypeStruct((groups, CAP * stations, own), bf16),
            jax.ShapeDtypeStruct((groups, own, CAP * stations), bf16),
        ),
        in_specs=[hbm] * 6,
        out_specs=(vmem,) * 4,
        scratch_shapes=[
            pltpu.SMEM((windows, own), jnp.int32),
            pltpu.SMEM(assign.shape, jnp.int32),
            pltpu.SMEM(target.shape, jnp.int32),
            pltpu.VMEM((comps, own, length), bf16),
            pltpu.VMEM(table.shape, bf16),
            pltpu.VMEM(band.shape, bf16),
            pltpu.SemaphoreType.DMA((5 + table.shape[0] // PART,)),
        ],
        compiler_params=room(0),
        name="front",
    )(*[pltpu.with_memory_space_constraint(v, pltpu.HBM) for v in operands])


def correlate_kernel(plan, owners, own, windows, base, kind, chunk_ref, *refs):
    refs = list(refs)
    self_ref, pick_ref, mine_ref, weight_ref, lag_ref = refs[:5]
    refs = refs[5:]
    sum_in = refs.pop(0) if kind["sums"] else None
    waiting = [(refs.pop(0), place) for place in kind["waiting"]]
    if kind["out_in"]:
        refs.pop(0)
    out_ref = refs.pop(0) if kind["out"] else None
    kept = refs.pop(0) if kind["keep"] else None
    sum_ref = refs.pop(0)
    rows_ref, picked, cross_e, result_e, cross, result, outv, energy_v, sem = refs
    me = lax.axis_index("pairs")
    pairs = GROUP * CAP
    stations = GROUP * own
    nine = COMP * COMP
    chunks = chunk_ref.shape[0] // stations
    total = sum_in[...] if kind["sums"] else jnp.zeros((own, nine * LANE), jnp.float32)

    def flush(source, place, which, ys=slice(None)):
        return [
            pltpu.make_async_copy(
                source.at[ys, j], out_ref.at[ys, owner_at(plan, me, place + j)], sem.at[which]
            )
            for j in range(GROUP)
        ]

    def copies(ch):
        return flush(outv.at[lax.rem(ch, 2)], base + ch * GROUP, lax.rem(ch, 2))

    before = [cp for source, place in waiting for cp in flush(source, place, 2)]
    for cp in before:
        cp.start()
    started = []

    def one_chunk(ch, total):
        slot = lax.rem(ch, 2)
        first_row = ch * stations if isinstance(ch, int) else pl.multiple_of(ch * stations, stations)
        here = pl.ds(first_row, stations)
        number = base // GROUP + ch
        each = one_hot(iota(own * pairs, own, 0) // pairs, own)
        spread = jnp.concatenate([each, mine_ref[number]], 0)
        rows_ref[...] = mm(spread, self_ref[...]).astype(jnp.bfloat16)
        picked[...] = mm(pick_ref[number], chunk_ref[here, :]).astype(jnp.bfloat16)

        def product(left, right):
            re = im = None
            for (lr, li), (rr, ri) in zip(left, right):
                r = lr * rr + li * ri
                i = li * rr - lr * ri
                re = r if re is None else re + r
                im = i if im is None else im + i
            return re, im

        def tile(load, a, lt):
            got = []
            for w in range(windows):
                both = []
                for part in range(2):
                    start = ((w * COMP + a) * 2 + part) * FREQ + lt * TILE
                    both.append(load(slice(start, start + TILE)))
                got.append(both)
            return got

        def partner(rows, lanes):
            return rows_ref[own * pairs + rows.start : own * pairs + rows.stop, lanes]

        tiles = FREQ // TILE

        def keep(ref, at, rows, lt, values):
            for part in range(2):
                start = (2 * lt + part) * TILE
                ref[at : at + rows, start : start + TILE] = values[part]

        for lt in range(tiles):
            lefts = [tile(lambda d: chunk_ref[here, d], a, lt) for a in range(COMP)]
            for c in range(CAP):
                part_rows = slice(c * stations, (c + 1) * stations)
                for b in range(COMP):
                    right = tile(lambda d: partner(part_rows, d), b, lt)
                    for a in range(COMP):
                        at = ((c * COMP + a) * COMP + b) * stations
                        keep(cross_e, at, stations, lt, product(lefts[a], right))
        result_e[...] = mm(cross_e[...], lag_ref[...])
        for lt in range(tiles):
            slots = [tile(lambda d: picked[:, d], b, lt) for b in range(COMP)]
            for yp in range(own // 2):
                y_rows = slice(yp * 2 * pairs, (yp + 1) * 2 * pairs)
                for a in range(COMP):
                    left = tile(lambda d: rows_ref[y_rows, d], a, lt)
                    for b in range(COMP):
                        at = ((yp * COMP + a) * COMP + b) * 2 * pairs
                        keep(cross, at, 2 * pairs, lt, product(left, slots[b]))
        result[...] = mm(cross[...], lag_ref[...])

        def flag_at(w):
            return slice(PLANE * windows + w * LANE, PLANE * windows + (w + 1) * LANE)

        squares = []
        for c in range(CAP):
            part_rows = slice(c * stations, (c + 1) * stations)
            count = None
            for w in range(windows):
                left = chunk_ref[here, flag_at(w)].astype(jnp.float32)
                term = left * partner(part_rows, flag_at(w)).astype(jnp.float32)
                count = term if count is None else count + term
            most = jnp.maximum(count, 1.0)
            share = 1.0 / (most * most * float(FREQ))
            lines = []
            for q in range(nine):
                at = (c * nine + q) * stations
                block = result_e[at : at + stations, :]
                square = block * block
                both = square[:, :LANE]
                for lt in range(1, LAGS // LANE):
                    both = both + square[:, lt * LANE : (lt + 1) * LANE]
                lines.append(both * share)
            squares.append(jnp.concatenate(lines, 1))
        total = total + mm(weight_ref[number], jnp.concatenate(squares, 0).astype(jnp.bfloat16))
        if kind["last"] and chunks == 1:
            finish(total)

        if not isinstance(ch, int):

            @pl.when(ch >= 2)
            def _():
                for cp in copies(ch):
                    cp.wait()

        for yp in range(own // 2):
            count = None
            for w in range(windows):
                left = rows_ref[yp * 2 * pairs : (yp + 1) * 2 * pairs, flag_at(w)].astype(jnp.float32)
                term = left * picked[:, flag_at(w)].astype(jnp.float32)
                count = term if count is None else count + term
            scale = 1.0 / (jnp.maximum(count, 1.0) * math.sqrt(FREQ))
            scale = jnp.concatenate([scale] * (LAGS // LANE), 1)
            ys = slice(2 * yp, 2 * yp + 2)
            for q in range(nine):
                at = (yp * nine + q) * 2 * pairs
                block = (result[at : at + 2 * pairs, :] * scale).astype(jnp.bfloat16)
                block = block.reshape(2, GROUP, CAP, LAGS)
                if kind["keep"]:
                    kept[ys, :, q, :, :] = block
                else:
                    outv[slot, ys, :, q, :, :] = block
            if chunks == 1 and not kind["keep"]:
                for cp in flush(outv.at[0], base, 0, ys):
                    cp.start()
                    started.append(cp)
        if chunks > 1:
            for cp in copies(ch):
                cp.start()
        return total

    def finish(total):
        lane = iota(own, nine, 1)
        energy = jnp.zeros((own, nine), jnp.float32)
        for q in range(nine):
            part = jnp.sum(total[:, q * LANE : (q + 1) * LANE], axis=1, keepdims=True)
            energy = jnp.where(lane == q, part, energy)
        energy_v[...] = energy / float(owners * LAGS)
        cp = pltpu.make_async_copy(energy_v, sum_ref, sem.at[3])
        cp.start()
        started.append(cp)

    if chunks == 1:
        total = one_chunk(0, total)
    else:
        total = lax.fori_loop(0, chunks, one_chunk, total)
        if kind["last"]:
            finish(total)
    if not kind["last"]:
        sum_ref[...] = total
    for cp in before + started:
        cp.wait()
    if chunks > 1:
        for ch in range(chunks - 2, chunks):
            for cp in copies(ch):
                cp.wait()


def correlate(plan, block, base, held, names, lags, carried, last, owners, windows):
    own = held.shape[0]
    nine = COMP * COMP
    stations, pairs = GROUP * own, GROUP * CAP
    vmem = pl.BlockSpec(memory_space=pltpu.VMEM)
    anywhere = pl.BlockSpec(memory_space=pl.ANY)
    f32, bf16 = jnp.float32, jnp.bfloat16
    chunks = block.shape[0] // stations
    sums, waiting, out_so_far = carried
    keep = chunks == 1 and not last
    kind = {
        "last": last,
        "sums": sums is not None,
        "waiting": [] if keep else [place for _, place in waiting],
        "out_in": out_so_far is not None and not keep,
        "keep": keep,
        "out": not keep,
    }
    operands, aliases = [block, held, *names, lags], {}
    specs = [vmem] * len(operands)
    if kind["sums"]:
        operands.append(sums)
        specs.append(vmem)
    if not keep:
        for source, _ in waiting:
            operands.append(source)
            specs.append(vmem)
        if out_so_far is not None:
            aliases = {len(operands): 0}
            operands.append(out_so_far)
            specs.append(anywhere)
    shapes, out_specs = [], []
    if kind["out"]:
        shapes.append(jax.ShapeDtypeStruct((own, owners, nine, CAP, LAGS), bf16))
        out_specs.append(anywhere)
    if keep:
        shapes.append(jax.ShapeDtypeStruct((own, GROUP, nine, CAP, LAGS), bf16))
        out_specs.append(vmem)
    shapes.append(jax.ShapeDtypeStruct((own, nine) if last else (own, nine * LANE), f32))
    out_specs.append(anywhere if last else vmem)
    half = CAP * nine * stations
    results = pl.pallas_call(
        functools.partial(correlate_kernel, plan, owners, own, windows, base, kind),
        out_shape=tuple(shapes),
        in_specs=specs,
        out_specs=tuple(out_specs),
        input_output_aliases=aliases,
        scratch_shapes=[
            pltpu.VMEM((own * pairs + CAP * stations, WIDE), bf16),
            pltpu.VMEM((2 * pairs, WIDE), bf16),
            pltpu.VMEM((half, 2 * FREQ), bf16),
            pltpu.VMEM((half, LAGS), f32),
            pltpu.VMEM((own * nine * pairs, 2 * FREQ), bf16),
            pltpu.VMEM((own * nine * pairs, LAGS), f32),
            pltpu.VMEM((2, own, GROUP, nine, CAP, LAGS), bf16),
            pltpu.VMEM((own, nine), f32),
            pltpu.SemaphoreType.DMA((4,)),
        ],
        compiler_params=room(2 * sum(v.size for v in operands[:-1])),
        cost_estimate=pl.CostEstimate(
            flops=chunks * 8 * half * FREQ * LAGS,
            bytes_accessed=chunks * 4 * half * LAGS,
            transcendentals=0,
        ),
        name="correlate",
    )(*operands)
    if keep:
        kept, sums = results
        return sums, waiting + [(kept, base)], out_so_far
    out, sums = results
    return sums, [], out


def steps_of(traces, gaps, assign, target):
    owners = lax.axis_size("pairs")
    own, windows = gaps.shape
    plan = exchange_plan(owners)
    lags = jnp.asarray(lag_table())

    def swap(block, mask):
        return lax.ppermute(block, "pairs", [(i, i ^ mask) for i in range(owners)])

    def join(*parts):
        return jnp.concatenate(parts, 0)

    held, *names = front(plan, traces, gaps, assign, target)
    wide, near, third = plan[:3]
    a = swap(held, wide)
    b0 = swap(held, near)
    b1 = swap(a, near)
    c0 = swap(join(held, a), third)
    c1 = swap(b0, third)
    c2 = swap(b1, third)
    blocks = [join(held, a, b0, b1)]
    other = [swap(blocks[0], 1)]
    if len(plan) > 3:
        blocks.append(join(c0, c1, c2))
        for mask in plan[3:]:
            blocks.append(swap(join(*blocks), mask))
        other += [swap(block, 1) for block in blocks[1:]]
    else:
        blocks.append(join(c0, c1, c2))
        far = [swap(c, 1) for c in (c0, c1, c2)]
        other.append(join(*far))
    base = 0
    order = []
    for block in blocks + other:
        order.append((block, base))
        base += block.shape[0] // own
    count = len(blocks)
    ranked = [order[i + side * count] for i in range(count) for side in range(2)]
    carried = (None, [], None)
    for at, (block, start) in enumerate(ranked):
        last = at == len(ranked) - 1
        carried = correlate(plan, block, start, held, names, lags, carried, last, owners, windows)
    energy, _, out = carried
    return out.transpose(0, 1, 3, 2, 4), energy


def solution(mesh):
    in_specs = (
        P(("groups", "pairs"), None, None),
        P(("groups", "pairs"), None),
        P("groups"),
        P("groups"),
    )
    out_specs = (P(("groups", "pairs"), None, None, None, None), P(("groups", "pairs"), None))
    return jax.shard_map(
        steps_of, mesh=mesh, in_specs=in_specs, out_specs=out_specs, check_vma=False
    )
```

```python
import functools
import math

import jax
import jax.numpy as jnp
import numpy as np
from jax import lax
from jax.experimental import pallas as pl
from jax.experimental.pallas import tpu as pltpu
from jax.sharding import PartitionSpec as P


SEG = 2048
FREQ = 512
FLO = 64
LAGS = 256
HALF = 21
CAP = 2
COMP = 3
RADIX = 4
LANE = 128
TILE = 2 * LANE
NONE = -1000
PART = SEG // RADIX
PLANE = 2 * COMP * FREQ
WINDOWS = 2
WIDE = WINDOWS * (PLANE + LANE)
GROUP = 4


def bin_order():
    spot = np.arange(FREQ)
    return RADIX * (spot % LANE) + spot // LANE


def dft_table():
    n1 = np.arange(PART)[:, None]
    blocks = []
    for r in range(RADIX):
        k = FLO + RADIX * np.arange(LANE)[None, :] + r
        phase = np.mod(n1 * k, SEG) * (2.0 * math.pi / SEG)
        blocks.append(np.concatenate([np.cos(phase), np.sin(phase)], 1))
    return np.concatenate(blocks, 0).astype(jnp.bfloat16)


def lag_table():
    bins = FLO + bin_order()[:, None]
    shifts = np.arange(LAGS)[None, :] - LAGS // 2
    phase = np.mod(bins * shifts, SEG) * (2.0 * math.pi / SEG)
    both = np.stack([np.cos(phase), -np.sin(phase)], 0).reshape(2, FREQ // TILE, TILE, LAGS)
    return both.transpose(1, 0, 2, 3).reshape(2 * FREQ, LAGS).astype(jnp.bfloat16)


def mm(a, b):
    return jnp.dot(a, b, preferred_element_type=jnp.float32)


def exchange_plan(count):
    bits = int(count).bit_length() - 1
    assert count == 1 << bits and bits >= 4
    chips = [1 << b for b in range(bits - 1, 0, -1)]
    return chips[:1] + chips[-1:] + chips[1:-1]


def owner_at(plan, me, place):
    mask = place >> len(plan)
    for i, m in enumerate(plan):
        mask = mask ^ (m * ((place >> i) & 1))
    return me ^ mask


def room(operand_bytes):
    return pltpu.CompilerParams(vmem_limit_bytes=(8 << 20) + operand_bytes)


def first_two(flags):
    found = [jnp.int32(NONE)] * CAP
    seen = jnp.int32(0)
    for s, flag in enumerate(flags):
        for c in range(CAP):
            found[c] = jnp.where(jnp.logical_and(flag, seen == c), s, found[c])
        seen = seen + flag.astype(jnp.int32)
    return found


def iota(rows, cols, dim):
    return lax.broadcasted_iota(jnp.int32, (rows, cols), dim)


def one_hot(want, cols):
    return jnp.where(iota(want.shape[0], cols, 1) == want, 1.0, 0.0).astype(jnp.bfloat16)


def meet(plan, own, assign_ref, target_ref, pick_ref, mine_ref, weight_ref):
    me = lax.axis_index("pairs")
    pairs = GROUP * CAP
    stations = GROUP * own
    place = iota(CAP * stations, own, 0)
    place = (place // stations) * GROUP + (place % stations) // own
    slot = iota(2 * pairs, stations, 0) % pairs
    col = iota(own, CAP * stations, 1)
    col = (col // stations) * GROUP + (col % stations) // own
    y_row = iota(own, CAP * stations, 0)
    my_target = target_ref[me]

    def one_group(ch, carry):
        want = jnp.full(place.shape, NONE, jnp.int32)
        taken = jnp.full(slot.shape, NONE, jnp.int32)
        weight = jnp.zeros(col.shape, jnp.float32)
        for j in range(GROUP):
            owner = owner_at(plan, me, ch * GROUP + j)
            wanted = target_ref[owner]
            mine = first_two([assign_ref[me * own + s] == wanted for s in range(own)])
            theirs = first_two([assign_ref[owner * own + s] == my_target for s in range(own)])
            for c in range(CAP):
                want = jnp.where(place == c * GROUP + j, mine[c], want)
                hit = jnp.logical_and(col == c * GROUP + j, y_row == mine[c])
                weight = jnp.where(hit, 1.0, weight)
                taken = jnp.where(slot == j * CAP + c, theirs[c] + j * own, taken)
        mine_ref[ch] = one_hot(want, own)
        pick_ref[ch] = one_hot(taken, stations)
        weight_ref[ch] = weight.astype(jnp.bfloat16)
        return carry

    lax.fori_loop(0, pick_ref.shape[0], one_group, 0)


def front_kernel(
    plan, gaps_hbm, assign_hbm, target_hbm, x_hbm, tab_hbm, out_ref, pick_ref, mine_ref,
    weight_ref, gaps_ref, assign_ref, target_ref, x_ref, tab_ref, sem,
):
    windows, own = gaps_ref.shape
    rows = windows * own
    parts = tab_ref.shape[0] // PART

    def part_at(i):
        return pl.ds(i * PART, PART)

    loads = [
        pltpu.make_async_copy(x_hbm, x_ref, sem.at[0]),
        *[
            pltpu.make_async_copy(tab_hbm.at[part_at(i)], tab_ref.at[part_at(i)], sem.at[1 + i])
            for i in range(parts)
        ],
        pltpu.make_async_copy(gaps_hbm, gaps_ref, sem.at[1 + parts]),
    ]
    names = [
        pltpu.make_async_copy(assign_hbm, assign_ref, sem.at[2 + parts]),
        pltpu.make_async_copy(target_hbm, target_ref, sem.at[3 + parts]),
    ]
    for load in names + loads:
        load.start()
    for load in names:
        load.wait()
    meet(plan, own, assign_ref, target_ref, pick_ref, mine_ref, weight_ref)
    loads[0].wait()
    quarter = []
    for j in range(RADIX):
        per_comp = []
        for a in range(COMP):
            pieces = [
                x_ref[a, :, w * SEG + j * PART : w * SEG + (j + 1) * PART].astype(jnp.float32)
                for w in range(windows)
            ]
            per_comp.append(jnp.concatenate(pieces, 0))
        quarter.append(jnp.concatenate(per_comp, 0))
    x0, x1, x2, x3 = quarter
    even, odd = x0 + x2, x1 + x3

    def halves(*ys):
        lows = [y - y.astype(jnp.bfloat16).astype(jnp.float32) for y in ys]
        return jnp.concatenate([*ys, *lows], 0).astype(jnp.bfloat16)

    def band(d):
        gap = RADIX * (iota(LANE, LANE, 0) - iota(LANE, LANE, 1)) + d
        return jnp.where(jnp.abs(gap) <= HALF, 1.0, 0.0).astype(jnp.bfloat16)

    bands = {d: band(d) for d in range(1 - RADIX, RADIX)}
    count = COMP * rows
    straight = [halves(even + odd), halves(even - odd)]
    turned = halves(x0 - x2, x1 - x3)

    def tab(i):
        loads[1 + i].wait()
        return tab_ref[part_at(i), :]

    spec = []
    for r in range(RADIX):
        if r % 2 == 0:
            d = mm(straight[r // 2], tab(r))
            d = d[:count] + d[count:]
            spec.append((d[:, :LANE], -d[:, LANE:]))
        else:
            d = mm(turned, tab(r))
            u = d[:count] + d[2 * count : 3 * count]
            v = d[count : 2 * count] + d[3 * count :]
            sign = 1.0 if r == 1 else -1.0
            spec.append(
                (u[:, :LANE] - sign * v[:, LANE:], -u[:, LANE:] - sign * v[:, :LANE])
            )
    power = []
    for re, im in spec:
        total = jnp.zeros((rows, LANE), jnp.float32)
        for a in range(COMP):
            both = re[a * rows : (a + 1) * rows], im[a * rows : (a + 1) * rows]
            total = total + (both[0] * both[0] + both[1] * both[1])
        power.append(total)
    power = jnp.concatenate(power, 1)
    p1 = power.astype(jnp.bfloat16).astype(jnp.float32)
    rest = power - p1
    p2 = rest.astype(jnp.bfloat16).astype(jnp.float32)
    p3 = rest - p2
    three = jnp.concatenate([p1, p2, p3], 0).astype(jnp.bfloat16)
    reach = [jnp.concatenate([bands[q - r] for r in range(RADIX)], 1) for q in range(RADIX)]
    sums = mm(three, jnp.concatenate(reach, 0))
    spot = iota(rows, FREQ, 1)
    f = RADIX * (spot % LANE) + spot // LANE
    taken = jnp.minimum(f + HALF, FREQ - 1) - jnp.maximum(f - HALF, 0) + 1
    share = 1.0 / (taken.astype(jnp.float32) * float(COMP))
    smooth = (sums[:rows] + sums[rows : 2 * rows] + sums[2 * rows :]) * share
    loads[1 + parts].wait()
    row_at = lax.broadcasted_iota(jnp.int32, (rows, LANE), 0)
    flags = jnp.zeros((rows, LANE), jnp.float32)
    for w in range(windows):
        for s in range(own):
            flags = jnp.where(row_at == w * own + s, gaps_ref[w, s].astype(jnp.float32), flags)
    wide_flags = jnp.concatenate([flags] * RADIX, 1)
    factor = wide_flags / jnp.sqrt(smooth + 1e-06)
    for a in range(COMP):
        for part in range(2):
            whole = jnp.concatenate([d[part][a * rows : (a + 1) * rows] for d in spec], 1)
            white = whole * factor
            for w in range(windows):
                start = w * PLANE + (2 * a + part) * FREQ
                out_ref[:, start : start + FREQ] = white[w * own : (w + 1) * own].astype(jnp.bfloat16)
    for w in range(windows):
        start = windows * PLANE + w * LANE
        out_ref[:, start : start + LANE] = flags[w * own : (w + 1) * own].astype(jnp.bfloat16)


def front(plan, traces, gaps, assign, target):
    own, comps, length = traces.shape
    windows = gaps.shape[1]
    assert comps == COMP and length == windows * SEG
    table = dft_table()
    operands = (gaps.T, assign, target, traces.transpose(1, 0, 2), jnp.asarray(table))
    hbm = pl.BlockSpec(memory_space=pltpu.HBM)
    vmem = pl.BlockSpec(memory_space=pltpu.VMEM)
    bf16 = jnp.bfloat16
    groups, stations = target.shape[0] // GROUP, GROUP * own
    return pl.pallas_call(
        functools.partial(front_kernel, plan),
        out_shape=(
            jax.ShapeDtypeStruct((own, windows * (PLANE + LANE)), bf16),
            jax.ShapeDtypeStruct((groups, 2 * GROUP * CAP, stations), bf16),
            jax.ShapeDtypeStruct((groups, CAP * stations, own), bf16),
            jax.ShapeDtypeStruct((groups, own, CAP * stations), bf16),
        ),
        in_specs=[hbm] * 5,
        out_specs=(vmem,) * 4,
        scratch_shapes=[
            pltpu.SMEM((windows, own), jnp.int32),
            pltpu.SMEM(assign.shape, jnp.int32),
            pltpu.SMEM(target.shape, jnp.int32),
            pltpu.VMEM((comps, own, length), bf16),
            pltpu.VMEM(table.shape, bf16),
            pltpu.SemaphoreType.DMA((4 + table.shape[0] // PART,)),
        ],
        compiler_params=room(0),
        name="front",
    )(*[pltpu.with_memory_space_constraint(v, pltpu.HBM) for v in operands])


def spread_kernel(mine_ref, self_ref, rows_ref, partner_ref):
    own = self_ref.shape[0]
    pairs = GROUP * CAP
    mine_rows = self_ref[...]
    each = one_hot(iota(own * pairs, own, 0) // pairs, own)
    rows_ref[...] = mm(each, mine_rows).astype(jnp.bfloat16)
    groups = mine_ref.shape[0]

    def one_group(ch, carry):
        partner_ref[ch] = mm(mine_ref[ch], mine_rows).astype(jnp.bfloat16)
        return carry

    lax.fori_loop(0, groups, one_group, 0, unroll=min(groups, 4))


def spread(held, mine):
    own, lanes = held.shape
    groups, made, _ = mine.shape
    vmem = pl.BlockSpec(memory_space=pltpu.VMEM)
    bf16 = jnp.bfloat16
    rows = own * GROUP * CAP
    total = rows + groups * made
    return pl.pallas_call(
        spread_kernel,
        out_shape=(
            jax.ShapeDtypeStruct((rows, lanes), bf16),
            jax.ShapeDtypeStruct((groups, made, lanes), bf16),
        ),
        in_specs=[vmem] * 2,
        out_specs=(vmem,) * 2,
        compiler_params=room(2 * total * lanes),
        cost_estimate=pl.CostEstimate(
            flops=2 * total * own * lanes, bytes_accessed=2 * total * lanes, transcendentals=0
        ),
        name="spread",
    )(mine, held)


def correlate_kernel(plan, owners, own, windows, base, kind, chunk_ref, *refs):
    refs = list(refs)
    rows_ref, partner_ref, pick_ref, weight_ref, lag_ref = refs[:5]
    refs = refs[5:]
    sum_in = refs.pop(0) if kind["sums"] else None
    waiting = [(refs.pop(0), place) for place in kind["waiting"]]
    if kind["out_in"]:
        refs.pop(0)
    out_ref = refs.pop(0) if kind["out"] else None
    kept = refs.pop(0) if kind["keep"] else None
    sum_ref = refs.pop(0)
    picked, cross_e, result_e, cross, result, outv, energy_v, sem = refs
    me = lax.axis_index("pairs")
    pairs = GROUP * CAP
    stations = GROUP * own
    nine = COMP * COMP
    chunks = chunk_ref.shape[0] // stations
    total = sum_in[...] if kind["sums"] else jnp.zeros((own, nine * LANE), jnp.float32)

    def flush(source, place, which, ys=slice(None)):
        return [
            pltpu.make_async_copy(
                source.at[ys, j], out_ref.at[ys, owner_at(plan, me, place + j)], sem.at[which]
            )
            for j in range(GROUP)
        ]

    def copies(ch):
        return flush(outv.at[lax.rem(ch, 2)], base + ch * GROUP, lax.rem(ch, 2))

    before = [cp for source, place in waiting for cp in flush(source, place, 2)]
    for cp in before:
        cp.start()
    started = []

    def one_chunk(ch, total):
        slot = lax.rem(ch, 2)
        first_row = ch * stations if isinstance(ch, int) else pl.multiple_of(ch * stations, stations)
        here = pl.ds(first_row, stations)
        number = base // GROUP + ch
        picked[...] = mm(pick_ref[number], chunk_ref[here, :]).astype(jnp.bfloat16)

        def product(left, right):
            re = im = None
            for (lr, li), (rr, ri) in zip(left, right):
                r = lr * rr + li * ri
                i = li * rr - lr * ri
                re = r if re is None else re + r
                im = i if im is None else im + i
            return re, im

        def tile(load, a, lt):
            got = []
            for w in range(windows):
                both = []
                for part in range(2):
                    start = ((w * COMP + a) * 2 + part) * FREQ + lt * TILE
                    both.append(load(slice(start, start + TILE)))
                got.append(both)
            return got

        def partner(rows, lanes):
            return partner_ref[number, rows, lanes]

        tiles = FREQ // TILE

        def keep(ref, at, rows, lt, values):
            for part in range(2):
                start = (2 * lt + part) * TILE
                ref[at : at + rows, start : start + TILE] = values[part]

        for c in range(CAP):
            part_rows = slice(c * stations, (c + 1) * stations)
            for lt in range(tiles):
                lefts = [tile(lambda d: chunk_ref[here, d], a, lt) for a in range(COMP)]
                for b in range(COMP):
                    right = tile(lambda d: partner(part_rows, d), b, lt)
                    for a in range(COMP):
                        at = ((c * COMP + a) * COMP + b) * stations
                        keep(cross_e, at, stations, lt, product(lefts[a], right))
            lines = slice(c * nine * stations, (c + 1) * nine * stations)
            result_e[lines, :] = mm(cross_e[lines, :], lag_ref[...])
        for yp in range(own // 2):
            y_rows = slice(yp * 2 * pairs, (yp + 1) * 2 * pairs)
            for lt in range(tiles):
                slots = [tile(lambda d: picked[:, d], b, lt) for b in range(COMP)]
                for a in range(COMP):
                    left = tile(lambda d: rows_ref[y_rows, d], a, lt)
                    for b in range(COMP):
                        at = ((yp * COMP + a) * COMP + b) * 2 * pairs
                        keep(cross, at, 2 * pairs, lt, product(left, slots[b]))
            lines = slice(yp * nine * 2 * pairs, (yp + 1) * nine * 2 * pairs)
            result[lines, :] = mm(cross[lines, :], lag_ref[...])

        def flag_at(w):
            return slice(PLANE * windows + w * LANE, PLANE * windows + (w + 1) * LANE)

        squares = []
        for c in range(CAP):
            part_rows = slice(c * stations, (c + 1) * stations)
            count = None
            for w in range(windows):
                left = chunk_ref[here, flag_at(w)].astype(jnp.float32)
                term = left * partner(part_rows, flag_at(w)).astype(jnp.float32)
                count = term if count is None else count + term
            most = jnp.maximum(count, 1.0)
            share = 1.0 / (most * most * float(FREQ))
            lines = []
            for q in range(nine):
                at = (c * nine + q) * stations
                block = result_e[at : at + stations, :]
                square = block * block
                both = square[:, :LANE]
                for lt in range(1, LAGS // LANE):
                    both = both + square[:, lt * LANE : (lt + 1) * LANE]
                lines.append(both * share)
            squares.append(jnp.concatenate(lines, 1))
        total = total + mm(weight_ref[number], jnp.concatenate(squares, 0).astype(jnp.bfloat16))
        if kind["last"] and chunks == 1:
            finish(total)

        if not isinstance(ch, int):

            @pl.when(ch >= 2)
            def _():
                for cp in copies(ch):
                    cp.wait()

        for yp in range(own // 2):
            count = None
            for w in range(windows):
                left = rows_ref[yp * 2 * pairs : (yp + 1) * 2 * pairs, flag_at(w)].astype(jnp.float32)
                term = left * picked[:, flag_at(w)].astype(jnp.float32)
                count = term if count is None else count + term
            scale = 1.0 / (jnp.maximum(count, 1.0) * math.sqrt(FREQ))
            scale = jnp.concatenate([scale] * (LAGS // LANE), 1)
            ys = slice(2 * yp, 2 * yp + 2)
            for q in range(nine):
                at = (yp * nine + q) * 2 * pairs
                block = (result[at : at + 2 * pairs, :] * scale).astype(jnp.bfloat16)
                block = block.reshape(2, GROUP, CAP, LAGS)
                if kind["keep"]:
                    kept[ys, :, q, :, :] = block
                else:
                    outv[slot, ys, :, q, :, :] = block
            if chunks == 1 and not kind["keep"]:
                for cp in flush(outv.at[0], base, 0, ys):
                    cp.start()
                    started.append(cp)
        if chunks > 1:
            for cp in copies(ch):
                cp.start()
        return total

    def finish(total):
        lane = iota(own, nine, 1)
        energy = jnp.zeros((own, nine), jnp.float32)
        for q in range(nine):
            part = jnp.sum(total[:, q * LANE : (q + 1) * LANE], axis=1, keepdims=True)
            energy = jnp.where(lane == q, part, energy)
        energy_v[...] = energy / float(owners * LAGS)
        cp = pltpu.make_async_copy(energy_v, sum_ref, sem.at[3])
        cp.start()
        started.append(cp)

    if chunks == 1:
        total = one_chunk(0, total)
    else:
        total = lax.fori_loop(0, chunks, one_chunk, total)
        if kind["last"]:
            finish(total)
    if not kind["last"]:
        sum_ref[...] = total
    for cp in before + started:
        cp.wait()
    if chunks > 1:
        for ch in range(chunks - 2, chunks):
            for cp in copies(ch):
                cp.wait()


def correlate(plan, block, base, rows, lags, carried, last, owners, windows):
    own = rows[3].shape[1]
    nine = COMP * COMP
    stations, pairs = GROUP * own, GROUP * CAP
    vmem = pl.BlockSpec(memory_space=pltpu.VMEM)
    anywhere = pl.BlockSpec(memory_space=pl.ANY)
    f32, bf16 = jnp.float32, jnp.bfloat16
    chunks = block.shape[0] // stations
    sums, waiting, out_so_far = carried
    keep = chunks == 1 and not last
    kind = {
        "last": last,
        "sums": sums is not None,
        "waiting": [] if keep else [place for _, place in waiting],
        "out_in": out_so_far is not None and not keep,
        "keep": keep,
        "out": not keep,
    }
    operands, aliases = [block, *rows, lags], {}
    specs = [vmem] * len(operands)
    if kind["sums"]:
        operands.append(sums)
        specs.append(vmem)
    if not keep:
        for source, _ in waiting:
            operands.append(source)
            specs.append(vmem)
        if out_so_far is not None:
            aliases = {len(operands): 0}
            operands.append(out_so_far)
            specs.append(anywhere)
    shapes, out_specs = [], []
    if kind["out"]:
        shapes.append(jax.ShapeDtypeStruct((own, owners, nine, CAP, LAGS), bf16))
        out_specs.append(anywhere)
    if keep:
        shapes.append(jax.ShapeDtypeStruct((own, GROUP, nine, CAP, LAGS), bf16))
        out_specs.append(vmem)
    shapes.append(jax.ShapeDtypeStruct((own, nine) if last else (own, nine * LANE), f32))
    out_specs.append(anywhere if last else vmem)
    half = CAP * nine * stations
    results = pl.pallas_call(
        functools.partial(correlate_kernel, plan, owners, own, windows, base, kind),
        out_shape=tuple(shapes),
        in_specs=specs,
        out_specs=tuple(out_specs),
        input_output_aliases=aliases,
        scratch_shapes=[
            pltpu.VMEM((2 * pairs, WIDE), bf16),
            pltpu.VMEM((half, 2 * FREQ), bf16),
            pltpu.VMEM((half, LAGS), f32),
            pltpu.VMEM((own * nine * pairs, 2 * FREQ), bf16),
            pltpu.VMEM((own * nine * pairs, LAGS), f32),
            pltpu.VMEM((2, own, GROUP, nine, CAP, LAGS), bf16),
            pltpu.VMEM((own, nine), f32),
            pltpu.SemaphoreType.DMA((4,)),
        ],
        compiler_params=room(2 * sum(v.size for v in operands[:-1])),
        cost_estimate=pl.CostEstimate(
            flops=chunks * 8 * half * FREQ * LAGS,
            bytes_accessed=chunks * 4 * half * LAGS,
            transcendentals=0,
        ),
        name="correlate",
    )(*operands)
    if keep:
        kept, sums = results
        return sums, waiting + [(kept, base)], out_so_far
    out, sums = results
    return sums, [], out


def steps_of(traces, gaps, assign, target):
    owners = lax.axis_size("pairs")
    own, windows = gaps.shape
    plan = exchange_plan(owners)
    lags = jnp.asarray(lag_table())

    def swap(block, mask):
        return lax.ppermute(block, "pairs", [(i, i ^ mask) for i in range(owners)])

    def join(*parts):
        return jnp.concatenate(parts, 0)

    held, pick, mine, weight = front(plan, traces, gaps, assign, target)
    rows = (*spread(held, mine), pick, weight)
    wide, near, third = plan[:3]
    a = swap(held, wide)
    b0 = swap(held, near)
    b1 = swap(a, near)
    c0 = swap(join(held, a), third)
    c1 = swap(b0, third)
    c2 = swap(b1, third)
    blocks = [join(held, a, b0, b1)]
    other = [swap(blocks[0], 1)]
    if len(plan) > 3:
        blocks.append(join(c0, c1, c2))
        for mask in plan[3:]:
            blocks.append(swap(join(*blocks), mask))
        other += [swap(block, 1) for block in blocks[1:]]
    else:
        blocks.append(join(c0, c1, c2))
        far = [swap(c, 1) for c in (c0, c1, c2)]
        other.append(join(*far))
    base = 0
    order = []
    for block in blocks + other:
        order.append((block, base))
        base += block.shape[0] // own
    count = len(blocks)
    ranked = [order[i + side * count] for i in range(count) for side in range(2)]
    carried = (None, [], None)
    for at, (block, start) in enumerate(ranked):
        last = at == len(ranked) - 1
        carried = correlate(plan, block, start, rows, lags, carried, last, owners, windows)
    energy, _, out = carried
    return out.transpose(0, 1, 3, 2, 4), energy


def solution(mesh):
    in_specs = (
        P(("groups", "pairs"), None, None),
        P(("groups", "pairs"), None),
        P("groups"),
        P("groups"),
    )
    out_specs = (P(("groups", "pairs"), None, None, None, None), P(("groups", "pairs"), None))
    return jax.shard_map(
        steps_of, mesh=mesh, in_specs=in_specs, out_specs=out_specs, check_vma=False
    )
```

```python
import functools
import math

import jax
import jax.numpy as jnp
import numpy as np
from jax import lax
from jax.experimental import pallas as pl
from jax.experimental.pallas import tpu as pltpu
from jax.sharding import PartitionSpec as P


SEG = 2048
FREQ = 512
FLO = 64
LAGS = 256
HALF = 21
CAP = 2
COMP = 3
RADIX = 4
LANE = 128
TILE = 2 * LANE
NONE = -1000
PART = SEG // RADIX
PLANE = 2 * COMP * FREQ
WINDOWS = 2
WIDE = WINDOWS * (PLANE + LANE)
GROUP = 4


def bin_order():
    spot = np.arange(FREQ)
    return RADIX * (spot % LANE) + spot // LANE


def dft_table():
    n1 = np.arange(PART)[:, None]
    blocks = []
    for r in range(RADIX):
        k = FLO + RADIX * np.arange(LANE)[None, :] + r
        phase = np.mod(n1 * k, SEG) * (2.0 * math.pi / SEG)
        blocks.append(np.concatenate([np.cos(phase), np.sin(phase)], 1))
    return np.concatenate(blocks, 0).astype(jnp.bfloat16)


def lag_table():
    bins = FLO + bin_order()[:, None]
    shifts = np.arange(LAGS)[None, :] - LAGS // 2
    phase = np.mod(bins * shifts, SEG) * (2.0 * math.pi / SEG)
    both = np.stack([np.cos(phase), -np.sin(phase)], 0).reshape(2, FREQ // TILE, TILE, LAGS)
    return both.transpose(1, 0, 2, 3).reshape(2 * FREQ, LAGS).astype(jnp.bfloat16)


def mm(a, b):
    return jnp.dot(a, b, preferred_element_type=jnp.float32)


def exchange_plan(count):
    bits = int(count).bit_length() - 1
    assert count == 1 << bits and bits >= 4
    chips = [1 << b for b in range(bits - 1, 0, -1)]
    return chips[:1] + chips[-1:] + chips[1:-1]


def owner_at(plan, me, place):
    mask = place >> len(plan)
    for i, m in enumerate(plan):
        mask = mask ^ (m * ((place >> i) & 1))
    return me ^ mask


def room(operand_bytes):
    return pltpu.CompilerParams(vmem_limit_bytes=(8 << 20) + operand_bytes)


def first_two(flags):
    found = [jnp.int32(NONE)] * CAP
    seen = jnp.int32(0)
    for s, flag in enumerate(flags):
        for c in range(CAP):
            found[c] = jnp.where(jnp.logical_and(flag, seen == c), s, found[c])
        seen = seen + flag.astype(jnp.int32)
    return found


def iota(rows, cols, dim):
    return lax.broadcasted_iota(jnp.int32, (rows, cols), dim)


def one_hot(want, cols):
    return jnp.where(iota(want.shape[0], cols, 1) == want, 1.0, 0.0).astype(jnp.bfloat16)


def meet(plan, own, assign_ref, target_ref, pick_ref, mine_ref, weight_ref, part, parts):
    me = lax.axis_index("pairs")
    pairs = GROUP * CAP
    stations = GROUP * own
    place = iota(CAP * stations, own, 0)
    place = (place // stations) * GROUP + (place % stations) // own
    slot = iota(2 * pairs, stations, 0) % pairs
    col = iota(own, CAP * stations, 1)
    col = (col // stations) * GROUP + (col % stations) // own
    y_row = iota(own, CAP * stations, 0)
    my_target = target_ref[me]

    def one_group(ch, carry):
        want = jnp.full(place.shape, NONE, jnp.int32)
        taken = jnp.full(slot.shape, NONE, jnp.int32)
        weight = jnp.zeros(col.shape, jnp.float32)
        for j in range(GROUP):
            owner = owner_at(plan, me, ch * GROUP + j)
            wanted = target_ref[owner]
            mine = first_two([assign_ref[me * own + s] == wanted for s in range(own)])
            theirs = first_two([assign_ref[owner * own + s] == my_target for s in range(own)])
            for c in range(CAP):
                want = jnp.where(place == c * GROUP + j, mine[c], want)
                hit = jnp.logical_and(col == c * GROUP + j, y_row == mine[c])
                weight = jnp.where(hit, 1.0, weight)
                taken = jnp.where(slot == j * CAP + c, theirs[c] + j * own, taken)
        mine_ref[ch] = one_hot(want, own)
        pick_ref[ch] = one_hot(taken, stations)
        weight_ref[ch] = weight.astype(jnp.bfloat16)
        return carry

    groups = pick_ref.shape[0]
    low, high = part * groups // parts, (part + 1) * groups // parts
    if high - low <= 2:
        for ch in range(low, high):
            one_group(ch, 0)
    else:
        lax.fori_loop(low, high, one_group, 0)


def front_kernel(
    plan, gaps_hbm, assign_hbm, target_hbm, x_hbm, tab_hbm, out_ref, pick_ref, mine_ref,
    weight_ref, gaps_ref, assign_ref, target_ref, x_ref, tab_ref, sem,
):
    windows, own = gaps_ref.shape
    rows = windows * own
    parts = tab_ref.shape[0] // PART

    def part_at(i):
        return pl.ds(i * PART, PART)

    loads = [
        pltpu.make_async_copy(x_hbm, x_ref, sem.at[0]),
        *[
            pltpu.make_async_copy(tab_hbm.at[part_at(i)], tab_ref.at[part_at(i)], sem.at[1 + i])
            for i in range(parts)
        ],
        pltpu.make_async_copy(gaps_hbm, gaps_ref, sem.at[1 + parts]),
    ]
    names = [
        pltpu.make_async_copy(assign_hbm, assign_ref, sem.at[2 + parts]),
        pltpu.make_async_copy(target_hbm, target_ref, sem.at[3 + parts]),
    ]
    for load in names + loads:
        load.start()
    loads[0].wait()
    for load in names:
        load.wait()
    who = functools.partial(meet, plan, own, assign_ref, target_ref, pick_ref, mine_ref, weight_ref)
    who(0, 2)
    quarter = []
    for j in range(RADIX):
        per_comp = []
        for a in range(COMP):
            pieces = [
                x_ref[a, :, w * SEG + j * PART : w * SEG + (j + 1) * PART].astype(jnp.float32)
                for w in range(windows)
            ]
            per_comp.append(jnp.concatenate(pieces, 0))
        quarter.append(jnp.concatenate(per_comp, 0))
    x0, x1, x2, x3 = quarter
    even, odd = x0 + x2, x1 + x3

    def halves(*ys):
        lows = [y - y.astype(jnp.bfloat16).astype(jnp.float32) for y in ys]
        return jnp.concatenate([*ys, *lows], 0).astype(jnp.bfloat16)

    def band(d):
        gap = RADIX * (iota(LANE, LANE, 0) - iota(LANE, LANE, 1)) + d
        return jnp.where(jnp.abs(gap) <= HALF, 1.0, 0.0).astype(jnp.bfloat16)

    bands = {d: band(d) for d in range(1 - RADIX, RADIX)}
    count = COMP * rows
    straight = [halves(even + odd), halves(even - odd)]
    turned = halves(x0 - x2, x1 - x3)

    for i in range(parts):
        loads[1 + i].wait()
    loads[1 + parts].wait()
    who(1, 2)

    def tab(i):
        return tab_ref[part_at(i), :]

    spec = []
    for r in range(RADIX):
        if r % 2 == 0:
            d = mm(straight[r // 2], tab(r))
            d = d[:count] + d[count:]
            spec.append((d[:, :LANE], -d[:, LANE:]))
        else:
            d = mm(turned, tab(r))
            u = d[:count] + d[2 * count : 3 * count]
            v = d[count : 2 * count] + d[3 * count :]
            sign = 1.0 if r == 1 else -1.0
            spec.append(
                (u[:, :LANE] - sign * v[:, LANE:], -u[:, LANE:] - sign * v[:, :LANE])
            )
    power = []
    for re, im in spec:
        total = jnp.zeros((rows, LANE), jnp.float32)
        for a in range(COMP):
            both = re[a * rows : (a + 1) * rows], im[a * rows : (a + 1) * rows]
            total = total + (both[0] * both[0] + both[1] * both[1])
        power.append(total)
    power = jnp.concatenate(power, 1)
    p1 = power.astype(jnp.bfloat16).astype(jnp.float32)
    rest = power - p1
    p2 = rest.astype(jnp.bfloat16).astype(jnp.float32)
    p3 = rest - p2
    three = jnp.concatenate([p1, p2, p3], 0).astype(jnp.bfloat16)
    reach = [jnp.concatenate([bands[q - r] for r in range(RADIX)], 1) for q in range(RADIX)]
    sums = mm(three, jnp.concatenate(reach, 0))
    spot = iota(rows, FREQ, 1)
    f = RADIX * (spot % LANE) + spot // LANE
    taken = jnp.minimum(f + HALF, FREQ - 1) - jnp.maximum(f - HALF, 0) + 1
    share = 1.0 / (taken.astype(jnp.float32) * float(COMP))
    smooth = (sums[:rows] + sums[rows : 2 * rows] + sums[2 * rows :]) * share
    row_at = lax.broadcasted_iota(jnp.int32, (rows, LANE), 0)
    flags = jnp.zeros((rows, LANE), jnp.float32)
    for w in range(windows):
        for s in range(own):
            flags = jnp.where(row_at == w * own + s, gaps_ref[w, s].astype(jnp.float32), flags)
    wide_flags = jnp.concatenate([flags] * RADIX, 1)
    factor = wide_flags / jnp.sqrt(smooth + 1e-06)
    for a in range(COMP):
        for part in range(2):
            whole = jnp.concatenate([d[part][a * rows : (a + 1) * rows] for d in spec], 1)
            white = whole * factor
            for w in range(windows):
                start = w * PLANE + (2 * a + part) * FREQ
                out_ref[:, start : start + FREQ] = white[w * own : (w + 1) * own].astype(jnp.bfloat16)
    for w in range(windows):
        start = windows * PLANE + w * LANE
        out_ref[:, start : start + LANE] = flags[w * own : (w + 1) * own].astype(jnp.bfloat16)


def front(plan, traces, gaps, assign, target):
    own, comps, length = traces.shape
    windows = gaps.shape[1]
    assert comps == COMP and length == windows * SEG
    table = dft_table()
    operands = (gaps.T, assign, target, traces.transpose(1, 0, 2), jnp.asarray(table))
    hbm = pl.BlockSpec(memory_space=pltpu.HBM)
    vmem = pl.BlockSpec(memory_space=pltpu.VMEM)
    bf16 = jnp.bfloat16
    groups, stations = target.shape[0] // GROUP, GROUP * own
    return pl.pallas_call(
        functools.partial(front_kernel, plan),
        out_shape=(
            jax.ShapeDtypeStruct((own, windows * (PLANE + LANE)), bf16),
            jax.ShapeDtypeStruct((groups, 2 * GROUP * CAP, stations), bf16),
            jax.ShapeDtypeStruct((groups, CAP * stations, own), bf16),
            jax.ShapeDtypeStruct((groups, own, CAP * stations), bf16),
        ),
        in_specs=[hbm] * 5,
        out_specs=(vmem,) * 4,
        scratch_shapes=[
            pltpu.SMEM((windows, own), jnp.int32),
            pltpu.SMEM(assign.shape, jnp.int32),
            pltpu.SMEM(target.shape, jnp.int32),
            pltpu.VMEM((comps, own, length), bf16),
            pltpu.VMEM(table.shape, bf16),
            pltpu.SemaphoreType.DMA((4 + table.shape[0] // PART,)),
        ],
        compiler_params=room(0),
        name="front",
    )(*[pltpu.with_memory_space_constraint(v, pltpu.HBM) for v in operands])


def spread_kernel(mine_ref, self_ref, rows_ref, partner_ref):
    own = self_ref.shape[0]
    pairs = GROUP * CAP
    mine_rows = self_ref[...]
    each = one_hot(iota(own * pairs, own, 0) // pairs, own)
    rows_ref[...] = mm(each, mine_rows).astype(jnp.bfloat16)
    groups = mine_ref.shape[0]

    def one_group(ch, carry):
        partner_ref[ch] = mm(mine_ref[ch], mine_rows).astype(jnp.bfloat16)
        return carry

    lax.fori_loop(0, groups, one_group, 0, unroll=min(groups, 4))


def spread(held, mine):
    own, lanes = held.shape
    groups, made, _ = mine.shape
    vmem = pl.BlockSpec(memory_space=pltpu.VMEM)
    bf16 = jnp.bfloat16
    rows = own * GROUP * CAP
    total = rows + groups * made
    return pl.pallas_call(
        spread_kernel,
        out_shape=(
            jax.ShapeDtypeStruct((rows, lanes), bf16),
            jax.ShapeDtypeStruct((groups, made, lanes), bf16),
        ),
        in_specs=[vmem] * 2,
        out_specs=(vmem,) * 2,
        compiler_params=room(2 * total * lanes),
        cost_estimate=pl.CostEstimate(
            flops=2 * total * own * lanes, bytes_accessed=2 * total * lanes, transcendentals=0
        ),
        name="spread",
    )(mine, held)


def correlate_kernel(plan, owners, own, windows, base, kind, chunk_ref, *refs):
    refs = list(refs)
    rows_ref, partner_ref, pick_ref, weight_ref, lag_ref = refs[:5]
    refs = refs[5:]
    sum_in = refs.pop(0) if kind["sums"] else None
    waiting = [(refs.pop(0), place) for place in kind["waiting"]]
    if kind["out_in"]:
        refs.pop(0)
    out_ref = refs.pop(0) if kind["out"] else None
    kept = refs.pop(0) if kind["keep"] else None
    sum_ref = refs.pop(0)
    picked, cross_e, result_e, cross, result, outv, energy_v, sem = refs
    me = lax.axis_index("pairs")
    pairs = GROUP * CAP
    stations = GROUP * own
    nine = COMP * COMP
    chunks = chunk_ref.shape[0] // stations
    total = sum_in[...] if kind["sums"] else jnp.zeros((own, nine * LANE), jnp.float32)

    def flush(source, place, which, ys=slice(None)):
        return [
            pltpu.make_async_copy(
                source.at[ys, j], out_ref.at[ys, owner_at(plan, me, place + j)], sem.at[which]
            )
            for j in range(GROUP)
        ]

    def copies(ch):
        return flush(outv.at[lax.rem(ch, 2)], base + ch * GROUP, lax.rem(ch, 2))

    before = [cp for source, place in waiting for cp in flush(source, place, 2)]
    for cp in before:
        cp.start()
    started = []

    def one_chunk(ch, total):
        slot = lax.rem(ch, 2)
        first_row = ch * stations if isinstance(ch, int) else pl.multiple_of(ch * stations, stations)
        here = pl.ds(first_row, stations)
        number = base // GROUP + ch
        picked[...] = mm(pick_ref[number], chunk_ref[here, :]).astype(jnp.bfloat16)

        def product(left, right):
            re = im = None
            for (lr, li), (rr, ri) in zip(left, right):
                r = lr * rr + li * ri
                i = li * rr - lr * ri
                re = r if re is None else re + r
                im = i if im is None else im + i
            return re, im

        def tile(load, a, lt):
            got = []
            for w in range(windows):
                both = []
                for part in range(2):
                    start = ((w * COMP + a) * 2 + part) * FREQ + lt * TILE
                    both.append(load(slice(start, start + TILE)))
                got.append(both)
            return got

        def partner(rows, lanes):
            return partner_ref[number, rows, lanes]

        tiles = FREQ // TILE

        def keep(ref, at, rows, lt, values):
            for part in range(2):
                start = (2 * lt + part) * TILE
                ref[at : at + rows, start : start + TILE] = values[part]

        for c in range(CAP):
            part_rows = slice(c * stations, (c + 1) * stations)
            for lt in range(tiles):
                lefts = [tile(lambda d: chunk_ref[here, d], a, lt) for a in range(COMP)]
                for b in range(COMP):
                    right = tile(lambda d: partner(part_rows, d), b, lt)
                    for a in range(COMP):
                        at = ((c * COMP + a) * COMP + b) * stations
                        keep(cross_e, at, stations, lt, product(lefts[a], right))
            lines = slice(c * nine * stations, (c + 1) * nine * stations)
            result_e[lines, :] = mm(cross_e[lines, :], lag_ref[...])
        for yp in range(own // 2):
            y_rows = slice(yp * 2 * pairs, (yp + 1) * 2 * pairs)
            for lt in range(tiles):
                slots = [tile(lambda d: picked[:, d], b, lt) for b in range(COMP)]
                for a in range(COMP):
                    left = tile(lambda d: rows_ref[y_rows, d], a, lt)
                    for b in range(COMP):
                        at = ((yp * COMP + a) * COMP + b) * 2 * pairs
                        keep(cross, at, 2 * pairs, lt, product(left, slots[b]))
            lines = slice(yp * nine * 2 * pairs, (yp + 1) * nine * 2 * pairs)
            result[lines, :] = mm(cross[lines, :], lag_ref[...])

        def flag_at(w):
            return slice(PLANE * windows + w * LANE, PLANE * windows + (w + 1) * LANE)

        squares = []
        for c in range(CAP):
            part_rows = slice(c * stations, (c + 1) * stations)
            count = None
            for w in range(windows):
                left = chunk_ref[here, flag_at(w)].astype(jnp.float32)
                term = left * partner(part_rows, flag_at(w)).astype(jnp.float32)
                count = term if count is None else count + term
            most = jnp.maximum(count, 1.0)
            share = 1.0 / (most * most * float(FREQ))
            lines = []
            for q in range(nine):
                at = (c * nine + q) * stations
                block = result_e[at : at + stations, :]
                square = block * block
                both = square[:, :LANE]
                for lt in range(1, LAGS // LANE):
                    both = both + square[:, lt * LANE : (lt + 1) * LANE]
                lines.append(both * share)
            squares.append(jnp.concatenate(lines, 1))
        total = total + mm(weight_ref[number], jnp.concatenate(squares, 0).astype(jnp.bfloat16))
        if not isinstance(ch, int):

            @pl.when(ch >= 2)
            def _():
                for cp in copies(ch):
                    cp.wait()

        for yp in range(own // 2):
            count = None
            for w in range(windows):
                left = rows_ref[yp * 2 * pairs : (yp + 1) * 2 * pairs, flag_at(w)].astype(jnp.float32)
                term = left * picked[:, flag_at(w)].astype(jnp.float32)
                count = term if count is None else count + term
            scale = 1.0 / (jnp.maximum(count, 1.0) * math.sqrt(FREQ))
            scale = jnp.concatenate([scale] * (LAGS // LANE), 1)
            ys = slice(2 * yp, 2 * yp + 2)
            for q in range(nine):
                at = (yp * nine + q) * 2 * pairs
                block = (result[at : at + 2 * pairs, :] * scale).astype(jnp.bfloat16)
                block = block.reshape(2, GROUP, CAP, LAGS)
                if kind["keep"]:
                    kept[ys, :, q, :, :] = block
                else:
                    outv[slot, ys, :, q, :, :] = block
            if chunks == 1 and not kind["keep"]:
                for cp in flush(outv.at[0], base, 0, ys):
                    cp.start()
                    started.append(cp)
        if chunks > 1:
            for cp in copies(ch):
                cp.start()
        return total

    def finish(total):
        lane = iota(own, nine, 1)
        energy = jnp.zeros((own, nine), jnp.float32)
        for q in range(nine):
            part = jnp.sum(total[:, q * LANE : (q + 1) * LANE], axis=1, keepdims=True)
            energy = jnp.where(lane == q, part, energy)
        energy_v[...] = energy / float(owners * LAGS)
        cp = pltpu.make_async_copy(energy_v, sum_ref, sem.at[3])
        cp.start()
        started.append(cp)

    if chunks == 1:
        total = one_chunk(0, total)
    else:
        total = lax.fori_loop(0, chunks, one_chunk, total)
    if kind["last"]:
        finish(total)
    if not kind["last"]:
        sum_ref[...] = total
    for cp in before + started:
        cp.wait()
    if chunks > 1:
        for ch in range(chunks - 2, chunks):
            for cp in copies(ch):
                cp.wait()


def correlate(plan, block, base, rows, lags, carried, last, owners, windows):
    own = rows[3].shape[1]
    nine = COMP * COMP
    stations, pairs = GROUP * own, GROUP * CAP
    vmem = pl.BlockSpec(memory_space=pltpu.VMEM)
    anywhere = pl.BlockSpec(memory_space=pl.ANY)
    f32, bf16 = jnp.float32, jnp.bfloat16
    chunks = block.shape[0] // stations
    sums, waiting, out_so_far = carried
    keep = chunks == 1 and not last
    kind = {
        "last": last,
        "sums": sums is not None,
        "waiting": [] if keep else [place for _, place in waiting],
        "out_in": out_so_far is not None and not keep,
        "keep": keep,
        "out": not keep,
    }
    operands, aliases = [block, *rows, lags], {}
    specs = [vmem] * len(operands)
    if kind["sums"]:
        operands.append(sums)
        specs.append(vmem)
    if not keep:
        for source, _ in waiting:
            operands.append(source)
            specs.append(vmem)
        if out_so_far is not None:
            aliases = {len(operands): 0}
            operands.append(out_so_far)
            specs.append(anywhere)
    shapes, out_specs = [], []
    if kind["out"]:
        shapes.append(jax.ShapeDtypeStruct((own, owners, nine, CAP, LAGS), bf16))
        out_specs.append(anywhere)
    if keep:
        shapes.append(jax.ShapeDtypeStruct((own, GROUP, nine, CAP, LAGS), bf16))
        out_specs.append(vmem)
    shapes.append(jax.ShapeDtypeStruct((own, nine) if last else (own, nine * LANE), f32))
    out_specs.append(anywhere if last else vmem)
    half = CAP * nine * stations
    results = pl.pallas_call(
        functools.partial(correlate_kernel, plan, owners, own, windows, base, kind),
        out_shape=tuple(shapes),
        in_specs=specs,
        out_specs=tuple(out_specs),
        input_output_aliases=aliases,
        scratch_shapes=[
            pltpu.VMEM((2 * pairs, WIDE), bf16),
            pltpu.VMEM((half, 2 * FREQ), bf16),
            pltpu.VMEM((half, LAGS), f32),
            pltpu.VMEM((own * nine * pairs, 2 * FREQ), bf16),
            pltpu.VMEM((own * nine * pairs, LAGS), f32),
            pltpu.VMEM((2, own, GROUP, nine, CAP, LAGS), bf16),
            pltpu.VMEM((own, nine), f32),
            pltpu.SemaphoreType.DMA((4,)),
        ],
        compiler_params=room(2 * sum(v.size for v in operands[:-1])),
        cost_estimate=pl.CostEstimate(
            flops=chunks * 8 * half * FREQ * LAGS,
            bytes_accessed=chunks * 4 * half * LAGS,
            transcendentals=0,
        ),
        name="correlate",
    )(*operands)
    if keep:
        kept, sums = results
        return sums, waiting + [(kept, base)], out_so_far
    out, sums = results
    return sums, [], out


def steps_of(traces, gaps, assign, target):
    owners = lax.axis_size("pairs")
    own, windows = gaps.shape
    plan = exchange_plan(owners)
    lags = jnp.asarray(lag_table())

    def swap(block, mask):
        return lax.ppermute(block, "pairs", [(i, i ^ mask) for i in range(owners)])

    def join(*parts):
        return jnp.concatenate(parts, 0)

    held, pick, mine, weight = front(plan, traces, gaps, assign, target)
    rows = (*spread(held, mine), pick, weight)
    wide, near, third = plan[:3]
    a = swap(held, wide)
    b0 = swap(held, near)
    b1 = swap(a, near)
    c0 = swap(join(held, a), third)
    c1 = swap(b0, third)
    c2 = swap(b1, third)
    blocks = [join(held, a, b0, b1)]
    other = [swap(blocks[0], 1)]
    if len(plan) > 3:
        blocks.append(join(c0, c1, c2))
        for mask in plan[3:]:
            blocks.append(swap(join(*blocks), mask))
        other += [swap(block, 1) for block in blocks[1:]]
    else:
        blocks.append(join(c0, c1, c2))
        far = [swap(c, 1) for c in (c0, c1, c2)]
        other.append(join(*far))
    base = 0
    order = []
    for block in blocks + other:
        order.append((block, base))
        base += block.shape[0] // own
    count = len(blocks)
    ranked = [order[i + side * count] for i in range(count) for side in range(2)]
    carried = (None, [], None)
    for at, (block, start) in enumerate(ranked):
        last = at == len(ranked) - 1
        carried = correlate(plan, block, start, rows, lags, carried, last, owners, windows)
    energy, _, out = carried
    return out.transpose(0, 1, 3, 2, 4), energy


def solution(mesh):
    in_specs = (
        P(("groups", "pairs"), None, None),
        P(("groups", "pairs"), None),
        P("groups"),
        P("groups"),
    )
    out_specs = (P(("groups", "pairs"), None, None, None, None), P(("groups", "pairs"), None))
    return jax.shard_map(
        steps_of, mesh=mesh, in_specs=in_specs, out_specs=out_specs, check_vma=False
    )
```
